32 devices in a mesh: sec: 4 (over z), tile: 8 (over y, x, core).
Axes of the slice: x: 2, y: 2, z: 4, core: 2. Of those that a mesh axis runs over, the one named last changes fastest.
Arguments:
- rendered: bfloat16 [8, 1024, 1024], P('tile', 'sec'), may hold values from -6 to 6
- cached: bfloat16 [4, 256, 25600], P('sec', 'tile'), may hold values from -6 to 6
- owners: int32 [4, 256, 1], P('sec', 'tile'), may hold values from 0 to 7; in each aligned block of 32 rows (0 to 31, 32 to 63, ..., all dimensions but the last counted through in order) at most 8 rows name the same one
- roots: int32 [4, 256, 2], P('sec', 'tile'), may hold values from 32 to 832
- offsets: int32 [4, 2], P('sec'), may hold values from -8 to 8
Outputs:
- corr_maps: bfloat16 [4, 8, 8, 8, 25600], P('sec', 'tile')
The draws below stay inside these ranges and needn't reach their ends.
Inputs may be any that keep to these rules, and one draw needn't show every extreme that they name: `owners`: among the 32 rows of one device, no tile owner is named more than 8 times, a bound that some block reaches.
All inputs are finite; a program needn't handle non-finite values.
Results may differ from the reference program's by a relative error of at most 0.0087.
Values may be sent and summed in bfloat16 or wider, within the bound.
A program may use at most 64 MiB of HBM per device.

```python
import math
import jax
import jax.numpy as jnp
import numpy as np
from jax import lax

P_SIZE = 160
R = 1024
SHIFT = 8
BLK_DEV = 32
HALF = 81
AREA = 25600
SECTIONS = 4
OWNERS = 8
CAP = 8
MARGIN = 32
BLOCKS = 256


def place_ends(drawn, own_key, least, high):
    spot = [jax.random.randint(jax.random.fold_in(own_key, axis), (), 0, length) for axis, length in enumerate(drawn.shape)]
    longest = drawn.shape.index(max(drawn.shape))
    neighbour = spot[:longest] + [(spot[longest] + 1) % drawn.shape[longest]] + spot[longest + 1:]
    return drawn.at[tuple(spot)].set(least).at[tuple(neighbour)].set(high)


def block_scale(key, dims, shards, low, high):
    def one(position, parts):
        heights = jax.random.uniform(jax.random.fold_in(jax.random.fold_in(key, 6), position), (parts,), jnp.float32, low / len(shards), high / len(shards))
        return jnp.repeat(jnp.exp(heights), dims[position] // parts).reshape((-1,) + (1,) * (len(dims) - position - 1))

    factor_of = one(*shards[0])
    for cut in shards[1:]:
        factor_of = factor_of * one(*cut)
    return factor_of


def routed_block(key, own, number, rows, count, top, bound, slope):
    order = jax.random.permutation(key, count)
    heavy_load, ordinary = load_shares(count, rows * top, bound, slope, True), load_shares(count, rows * top, bound, slope, False)
    places = jnp.arange(count)

    def named(lengths, offset_by):
        used = int((lengths > 0).sum())
        fixed = max(1, used // 4)
        passed = fixed + (places - fixed + offset_by * (used - fixed)) % max(1, count - fixed)
        return jnp.zeros((count,), jnp.int32).at[order[jnp.where(places < fixed, places, passed)]].set(jnp.asarray(lengths, jnp.int32))

    lengths = jnp.where(number % 4 == 0, named(heavy_load, number // 4), named(ordinary, number - number // 4 - 1))
    mixed = jax.random.permutation(jax.random.fold_in(own, 3), count)
    giver, receiver = mixed[0:count // 2 * 2:2], mixed[1:count // 2 * 2:2]
    margin = jnp.minimum(lengths[giver] - 1, bound - lengths[receiver]) // 2
    margin = jnp.where((giver == order[0]) | (receiver == order[0]) | (lengths[receiver] == 0), 0, jnp.maximum(margin, 0))
    passed = jax.random.randint(jax.random.fold_in(own, 4), (count // 2,), 0, 1 << 20) % (margin + 1)
    lengths = lengths.at[giver].add(-passed).at[receiver].add(passed)
    items = jnp.searchsorted(jnp.cumsum(lengths), jnp.arange(rows * top), side="right").astype(jnp.int32)
    grid = items.reshape(top, rows).T
    grid = grid[jax.random.permutation(jax.random.fold_in(own, 1), rows)]
    offset_by = jax.random.randint(jax.random.fold_in(own, 2), (rows, 1), 0, top)
    return jnp.take_along_axis(grid, (jnp.arange(top)[None, :] + offset_by) % top, axis=1)


def load_shares(number_of, total, most, lean, full):
    portions = [(1 << 20) // math.isqrt(rank ** lean) + 1 for rank in range(1, number_of + 1)]
    largest = most if full else min(most, max(-(-total // number_of), total * portions[0] // sum(portions)))
    least = 1 if total - largest >= number_of - 1 else 0
    given, spare = [largest] + [least] * (number_of - 1), total - largest - least * (number_of - 1)
    while spare > 0:
        movable = [i for i in range(1, number_of) if given[i] < largest] or [i for i in range(1, number_of) if given[i] < most]
        pool, remaining = sum([portions[i] for i in movable]), spare
        for i in movable:
            more = min(most - given[i], max(1, remaining * portions[i] // pool), spare)
            given[i] = given[i] + more
            spare = spare - more
    return np.array(given)


def bell_draw(key, dims, scale, limit, pieces=(), kind=jnp.bfloat16):
    entries = jax.random.normal(key, dims, jnp.float32) * scale
    if len(pieces) > 0:
        entries = block_scale(key, dims, pieces, -0.22, 0.18) * entries
    return jnp.clip(entries, min=-limit, max=limit).astype(kind)


def setup_inputs(seed: int = 0) -> dict:
    streams_of = jax.random.split(jax.random.key(seed), 6)
    rendered = bell_draw(streams_of[0], (OWNERS, R, R), 1.0, 6.0, ((0, 8), (1, 4)))
    cached = bell_draw(streams_of[1], (SECTIONS, BLOCKS, AREA), 1.0, 6.0, ((0, 4), (1, 8)))
    owners_keys = jax.random.split(jax.random.fold_in(streams_of[2], 1), SECTIONS * BLOCKS // BLK_DEV)
    owners_turns = jax.random.permutation(jax.random.fold_in(streams_of[2], 3), SECTIONS * BLOCKS // BLK_DEV)
    owners = jax.vmap(lambda own, number: routed_block(jax.random.fold_in(streams_of[2], 2), own, number, BLK_DEV, OWNERS, 1, CAP, 2))(owners_keys, owners_turns).reshape((SECTIONS, BLOCKS, 1))
    roots = place_ends(jax.random.randint(streams_of[3], (SECTIONS, BLOCKS, 2), MARGIN, R - P_SIZE - MARGIN + 1), jax.random.fold_in(streams_of[3], 1), MARGIN, R - P_SIZE - MARGIN).astype(jnp.int32)
    offsets = place_ends(jax.random.randint(streams_of[4], (SECTIONS, 2), 0 - SHIFT, SHIFT + 1), jax.random.fold_in(streams_of[4], 1), 0 - SHIFT, SHIFT).astype(jnp.int32)
    return {"rendered": rendered, "cached": cached, "owners": owners, "roots": roots, "offsets": offsets}


def dft_tables():
    full_idx = jnp.arange(P_SIZE, dtype=jnp.int32)
    half_idx = jnp.arange(HALF, dtype=jnp.int32)
    full_phase = ((full_idx[:, None] * full_idx[None, :]) % P_SIZE).astype(jnp.float32) * (2.0 * math.pi / P_SIZE)
    half_phase = ((full_idx[:, None] * half_idx[None, :]) % P_SIZE).astype(jnp.float32) * (2.0 * math.pi / P_SIZE)
    right = jnp.concatenate([jnp.cos(half_phase), -jnp.sin(half_phase)], axis=1).astype(jnp.bfloat16)
    left = jnp.concatenate([jnp.cos(full_phase), jnp.sin(full_phase)], axis=1).astype(jnp.bfloat16)
    counts = jnp.where((half_idx == 0) | (half_idx == P_SIZE // 2), 1.0, 2.0).astype(jnp.float32)
    scaled = counts[:, None] / P_SIZE
    back = jnp.concatenate([scaled * jnp.cos(half_phase).T, -scaled * jnp.sin(half_phase).T], axis=0).astype(jnp.bfloat16)
    return right, left, back, counts


def spectrum(patches, right, left):
    segment = jnp.einsum('sjl,lm->sjm', patches.astype(jnp.float32), right.astype(jnp.float32)).astype(jnp.bfloat16)
    swapped = jnp.concatenate([segment[:, :, HALF:], -segment[:, :, :HALF]], axis=2)
    stacked = jnp.concatenate([segment, swapped], axis=1)
    return jnp.einsum('kj,sjm->skm', left.astype(jnp.float32), stacked.astype(jnp.float32)).astype(jnp.bfloat16)


def sharpened(moving, template_spec, left, back, counts):
    move_re = moving[:, :, :HALF].astype(jnp.float32)
    move_im = moving[:, :, HALF:].astype(jnp.float32)
    tmpl_re = template_spec[:, :, :HALF].astype(jnp.float32)
    tmpl_im = template_spec[:, :, HALF:].astype(jnp.float32)
    cross_re = move_re * tmpl_re + move_im * tmpl_im
    cross_im = move_im * tmpl_re - move_re * tmpl_im
    energy = 0.5 * (move_re * move_re + move_im * move_im + tmpl_re * tmpl_re + tmpl_im * tmpl_im)
    mean_power = jnp.sum(energy * counts, axis=(1, 2)) / (P_SIZE * P_SIZE)
    divisor = energy + 0.1 * mean_power[:, None, None] + 1e-5
    whitened = jnp.concatenate([cross_re / divisor, cross_im / divisor], axis=2).astype(jnp.bfloat16)
    swapped = jnp.concatenate([-whitened[:, :, HALF:], whitened[:, :, :HALF]], axis=2)
    stacked = jnp.concatenate([whitened, swapped], axis=1)
    rotated = jnp.einsum('kj,sjm->skm', left.astype(jnp.float32), stacked.astype(jnp.float32)).astype(jnp.bfloat16)
    result = jnp.einsum('sjm,ml->sjl', rotated.astype(jnp.float32), back.astype(jnp.float32)).astype(jnp.bfloat16)
    return result.reshape(result.shape[0], P_SIZE * P_SIZE)


def slot_ranks(target):
    positions = jnp.arange(target.shape[0], dtype=jnp.int32)
    earlier = (target[:, None] == target[None, :]) & (positions[None, :] < positions[:, None])
    return jnp.sum(earlier.astype(jnp.int32), axis=1).astype(jnp.int32)


def reference(rendered, cached, owners, roots, offsets):
    right, left, back, counts = dft_tables()
    drift_sum = jnp.cumsum(offsets, axis=0).astype(jnp.int32)

    def per_group(group_index):
        section = (group_index // OWNERS).astype(jnp.int32)
        source = (group_index % OWNERS).astype(jnp.int32)
        first_row = (source * BLK_DEV).astype(jnp.int32)
        root_zero = jnp.zeros((), jnp.int32)
        blocks = lax.dynamic_slice(cached, (section, first_row, root_zero), (1, BLK_DEV, AREA))[0]
        target = lax.dynamic_slice(owners, (section, first_row, root_zero), (1, BLK_DEV, 1))[0, :, 0]
        root_rows = lax.dynamic_slice(roots, (section, first_row, root_zero), (1, BLK_DEV, 2))[0]
        drift_now = lax.dynamic_slice(drift_sum, (section, root_zero), (1, 2))[0]
        top_rows = (root_rows[:, 0] + drift_now[0]).astype(jnp.int32)
        left_cols = (root_rows[:, 1] + drift_now[1]).astype(jnp.int32)

        def cut_window(owner_id, row_start, col_start):
            return lax.dynamic_slice(rendered, (owner_id, row_start, col_start), (1, P_SIZE, P_SIZE))[0]

        templates = jax.vmap(cut_window)(target, top_rows, left_cols)
        moving = spectrum(blocks.reshape(BLK_DEV, P_SIZE, P_SIZE), right, left)
        template_spec = spectrum(templates, right, left)
        return sharpened(moving, template_spec, left, back, counts), slot_ranks(target), target

    corr, slots, targets = lax.map(per_group, jnp.arange(SECTIONS * OWNERS, dtype=jnp.int32))
    group_ids = jnp.repeat(jnp.arange(SECTIONS * OWNERS, dtype=jnp.int32), BLK_DEV)
    section_ids = (group_ids // OWNERS).astype(jnp.int32)
    source_ids = (group_ids % OWNERS).astype(jnp.int32)
    result_maps = jnp.zeros((SECTIONS, OWNERS, OWNERS, CAP, AREA), jnp.bfloat16)
    result_maps = result_maps.at[section_ids, targets.reshape(-1), source_ids, slots.reshape(-1)].set(corr.reshape(-1, AREA))
    return result_maps
```

```python
import functools
import math

import jax
import jax.numpy as jnp
import ml_dtypes
import numpy as np
from jax import lax
from jax.experimental import pallas as pl
from jax.experimental.pallas import tpu as pltpu
from jax.sharding import PartitionSpec as P

LANES = 128
BATCH = 4


def tables(side):
    half = side // 2 + 1
    pad = -(-half // 8) * 8
    group = side // 32 - 1
    count = side // group
    full = np.arange(side)
    low = np.arange(half)
    phase = (full[:, None] * low[None, :] % side).astype(np.float32) * np.float32(2.0 * math.pi / side)
    cos = np.cos(phase).astype(ml_dtypes.bfloat16)
    sin = np.sin(phase).astype(ml_dtypes.bfloat16)
    counts = np.where((low == 0) | (low == side // 2), 1.0, 2.0).astype(np.float32)
    right = np.zeros((side, 2 * LANES), ml_dtypes.bfloat16)
    right[:, :half] = cos
    right[:, LANES : LANES + half] = -sin
    back = np.zeros((2 * LANES, side), ml_dtypes.bfloat16)
    scaled = counts[:, None] / np.float32(side)
    back[:half] = (scaled * np.cos(phase).T).astype(ml_dtypes.bfloat16)
    back[LANES : LANES + half] = (-scaled * np.sin(phase).T).astype(ml_dtypes.bfloat16)
    order = (np.arange(count)[None, :] * group + np.arange(group)[:, None]).reshape(-1)
    left_t = np.zeros((2 * pad, side), ml_dtypes.bfloat16)
    left_t[:half] = cos.T
    left_t[pad : pad + half] = sin.T
    left_m = left_t[:, order]
    left_i = left_m.T.copy()
    right_m = np.zeros((group, 2 * LANES, 2 * LANES), ml_dtypes.bfloat16)
    back_m = np.zeros((group, 2 * LANES, 2 * LANES), ml_dtypes.bfloat16)
    for r in range(group):
        at = side * r - LANES * r
        right_m[r, at : at + side] = right
        back_m[r, :, at : at + side] = back
    power = np.zeros((2, pad, LANES), np.float32)
    power[:, :half, :half] = counts[None, None, :]
    power[1, 0] = 0.0
    power[1, side // 2] = 0.0
    return right, right_m, left_t, left_m, left_i, back_m, power


def correlate(side, slots, flat_chunks, group, count, pad, roots, drift, flat, anchor_in, right, right_m,
              left_t, left_m, left_i, back_m, power, out, pix, anchor, todo):
    chunks = group + 1
    f32, bf16 = jnp.float32, jnp.bfloat16
    rows_in, width = anchor_in.shape

    def widen(i, carry):
        at = pl.multiple_of(i * 32, 32)
        for c in range(width // LANES):
            wide = anchor_in[pl.ds(at, 32), c * LANES : (c + 1) * LANES].astype(f32)
            anchor[pl.ds(at + c * rows_in, 32), :] = wide
        return carry

    lax.fori_loop(0, rows_in // 32, widen, 0)

    def spread(i, carry):
        for u in range(8):
            t = i * 8 + u
            at = pl.multiple_of(t * LANES, LANES)
            for g in range(slots // 16):
                part = flat[g * 16 : g * 16 + 16, pl.ds(at, LANES)].astype(f32)
                pix[pl.ds(g * 16 * flat_chunks + t, 8, stride=flat_chunks), :] = part[:8]
                pix[pl.ds((g * 16 + 8) * flat_chunks + t, 8, stride=flat_chunks), :] = part[8:]
        return carry

    lax.fori_loop(0, flat_chunks // 8, spread, 0)

    def listed(i, used):
        todo[used] = i
        return used + (roots[i, 0] > 0).astype(jnp.int32)

    used = lax.fori_loop(0, slots, listed, jnp.int32(0))
    for u in range(BATCH):
        todo[used + u] = slots

    lane = lax.broadcasted_iota(jnp.int32, (side, LANES), 1)

    def mm(a, b):
        return jnp.dot(a, b, preferred_element_type=f32)

    def window(slot):
        here = jnp.minimum(slot, slots - 1)
        row = jnp.clip(roots[here, 0] + drift[0, 0], 0, rows_in - side)
        col = jnp.clip(roots[here, 1] + drift[0, 1], 0, width - side)
        chunk = col // LANES
        off = col - chunk * LANES
        turn = lax.rem(LANES - off, LANES)
        pieces = []
        for u in range(3):
            at = jnp.minimum(chunk + u, width // LANES - 1) * rows_in + row
            pieces.append(pltpu.roll(anchor[pl.ds(at, side), :], turn, 1))
        keep = lane < LANES - off
        first = jnp.where(keep, pieces[0], pieces[1])
        second = jnp.where(keep, pieces[1], pieces[2])
        return jnp.concatenate([first, second], axis=1)[:, :side].astype(bf16)

    def halves(left, segment):
        both = mm(left, segment)
        p_re, p_im = both[:pad, :LANES], both[:pad, LANES:]
        q_re, q_im = both[pad:, :LANES], both[pad:, LANES:]
        return [
            x.astype(bf16).astype(f32)
            for x in (p_re + q_im, p_im - q_re, p_re - q_im, p_im + q_re)
        ]

    def batch(i, carry):
        ids = [todo[i * BATCH + u] for u in range(BATCH)]
        pieces = [
            [pix[pl.ds(s * flat_chunks + q, count, stride=chunks), :] for q in range(chunks)] for s in ids
        ]
        seg = []
        for r in range(group):
            lhs = jnp.concatenate(
                [jnp.concatenate([x[r], x[r + 1]], axis=1) for x in pieces], axis=0
            ).astype(bf16)
            seg.append(mm(lhs, right_m[r]))
        wins = jnp.concatenate([window(s) for s in ids], axis=0)
        seg_t = mm(wins, right[...]).astype(bf16)
        turned = []
        for u in range(BATCH):
            seg_m = jnp.concatenate([x[u * count : (u + 1) * count] for x in seg], axis=0).astype(bf16)
            move = halves(left_m[...], seg_m)
            tmpl = halves(left_t[...], seg_t[u * side : (u + 1) * side])
            energy, cross = [], []
            for h in range(2):
                a_re, a_im = move[2 * h], move[2 * h + 1]
                b_re, b_im = tmpl[2 * h], tmpl[2 * h + 1]
                cross.append((a_re * b_re + a_im * b_im, a_im * b_re - a_re * b_im))
                energy.append(0.5 * (a_re * a_re + a_im * a_im + b_re * b_re + b_im * b_im))
            total = jnp.sum(energy[0] * power[0] + energy[1] * power[1])
            floor = 0.1 * (total / (side * side)) + 1e-05
            white = []
            for h in range(2):
                inverse = 1.0 / (energy[h] + floor)
                pair = [(x * inverse).astype(bf16).astype(f32) for x in cross[h]]
                if h == 1:
                    pair = [jnp.where(edge, x, 0.0) for x in pair]
                white.append(pair)
            (p_re, p_im), (m_re, m_im) = white
            rhs = jnp.concatenate(
                [
                    jnp.concatenate([p_re + m_re, p_im + m_im], axis=1),
                    jnp.concatenate([m_im - p_im, p_re - m_re], axis=1),
                ],
                axis=0,
            ).astype(bf16)
            turned.append(mm(left_i[...], rhs))
        prior = None
        for r in range(group):
            lhs = jnp.concatenate([x[r * count : (r + 1) * count] for x in turned], axis=0).astype(bf16)
            got = mm(lhs, back_m[r])
            now = got[:, :LANES] if prior is None else prior + got[:, :LANES]
            for u, s in enumerate(ids):
                pix[pl.ds(s * flat_chunks + r, count, stride=chunks), :] = now[u * count : (u + 1) * count]
            prior = got[:, LANES:]
        for u, s in enumerate(ids):
            pix[pl.ds(s * flat_chunks + group, count, stride=chunks), :] = prior[u * count : (u + 1) * count]
        return carry

    at_row = lax.broadcasted_iota(jnp.int32, (pad, LANES), 0)
    edge = (at_row != 0) & (at_row != side // 2)
    lax.fori_loop(0, (used + BATCH - 1) // BATCH, batch, 0)

    def gather(i, carry):
        for u in range(8):
            t = i * 8 + u
            at = pl.multiple_of(t * LANES, LANES)
            for g in range(slots // 16):
                low = pix[pl.ds(g * 16 * flat_chunks + t, 8, stride=flat_chunks), :]
                high = pix[pl.ds((g * 16 + 8) * flat_chunks + t, 8, stride=flat_chunks), :]
                out[g * 16 : g * 16 + 16, pl.ds(at, LANES)] = jnp.concatenate([low, high], axis=0).astype(bf16)
        return carry

    lax.fori_loop(0, flat_chunks // 8, gather, 0)


def sharpened(flat, root_rows, drift_now, anchor):
    slots, area = flat.shape
    side = math.isqrt(area)
    consts = tables(side)
    group = consts[1].shape[0]
    pad = consts[6].shape[1]
    flat_chunks = area // LANES
    vmem = pl.BlockSpec(memory_space=pltpu.VMEM)
    smem = pl.BlockSpec(memory_space=pltpu.SMEM)
    return pl.pallas_call(
        functools.partial(correlate, side, slots, flat_chunks, group, side // group, pad),
        out_shape=jax.ShapeDtypeStruct((slots, area), jnp.bfloat16),
        in_specs=[smem, smem] + [vmem] * 9,
        out_specs=vmem,
        scratch_shapes=[
            pltpu.VMEM(((slots + 1) * flat_chunks, LANES), jnp.float32),
            pltpu.VMEM((anchor.size // LANES, LANES), jnp.float32),
            pltpu.SMEM((slots + BATCH + 1,), jnp.int32),
        ],
        compiler_params=pltpu.CompilerParams(vmem_limit_bytes=48 << 20),
        name="correlate",
    )(root_rows, drift_now, flat, anchor, *[jnp.asarray(x) for x in consts])


def slot_ranks(target):
    positions = jnp.arange(target.shape[0], dtype=jnp.int32)
    earlier = (target[:, None] == target[None, :]) & (positions[None, :] < positions[:, None])
    return jnp.sum(earlier.astype(jnp.int32), axis=1)


def body(rendered, cached, owners, roots, offsets):
    area = cached.shape[2]
    held = cached.shape[1]
    steps = lax.all_gather(offsets[0], "sec")
    place = lax.axis_index("sec")
    drift_now = jnp.sum(
        jnp.where(jnp.arange(steps.shape[0])[:, None] <= place, steps, 0), axis=0, keepdims=True
    )
    anchor = lax.all_gather(rendered, "sec", axis=1, tiled=True)[0]
    owner_count = lax.axis_size("tile")
    capacity = max(2, 2 * held // owner_count)
    target = owners[0, :, 0]
    slot_place = target * capacity + slot_ranks(target)
    slots_all = jnp.arange(owner_count * capacity, dtype=jnp.int32)
    selector = slots_all[:, None] == slot_place[None, :]
    root_send = jnp.sum(jnp.where(selector[:, :, None], roots[0][None, :, :], 0), axis=1)
    root_send = root_send.reshape(owner_count, capacity, 2)
    packed = jnp.dot(selector.astype(jnp.bfloat16), cached[0], preferred_element_type=jnp.float32)
    packed = packed.astype(jnp.bfloat16).reshape(owner_count, capacity, area)
    payload = lax.all_to_all(packed, "tile", split_axis=0, concat_axis=0, tiled=True)
    root_rows = lax.all_to_all(root_send, "tile", split_axis=0, concat_axis=0, tiled=True)
    result = sharpened(payload.reshape(-1, area), root_rows.reshape(-1, 2), drift_now, anchor)
    return result.reshape(1, 1, owner_count, capacity, area)


def solution(mesh):
    placed = (
        P("tile", "sec", None),
        P("sec", "tile", None),
        P("sec", "tile", None),
        P("sec", "tile", None),
        P("sec", None),
    )
    return jax.shard_map(
        body,
        mesh=mesh,
        in_specs=placed,
        out_specs=P("sec", "tile", None, None, None),
        check_vma=False,
    )
```

```python
import functools
import math

import jax
import jax.numpy as jnp
import ml_dtypes
import numpy as np
from jax import lax
from jax.experimental import pallas as pl
from jax.experimental.pallas import tpu as pltpu
from jax.sharding import PartitionSpec as P

LANES = 128
BATCH = 4
MESH = pl.DeviceIdType.MESH


def tables(side):
    half = side // 2 + 1
    pad = -(-half // 8) * 8
    group = side // 32 - 1
    count = side // group
    full = np.arange(side)
    low = np.arange(half)
    phase = (full[:, None] * low[None, :] % side).astype(np.float32) * np.float32(2.0 * math.pi / side)
    cos = np.cos(phase).astype(ml_dtypes.bfloat16)
    sin = np.sin(phase).astype(ml_dtypes.bfloat16)
    counts = np.where((low == 0) | (low == side // 2), 1.0, 2.0).astype(np.float32)
    right = np.zeros((side, 2 * LANES), ml_dtypes.bfloat16)
    right[:, :half] = cos
    right[:, LANES : LANES + half] = -sin
    back = np.zeros((2 * LANES, side), ml_dtypes.bfloat16)
    scaled = counts[:, None] / np.float32(side)
    back[:half] = (scaled * np.cos(phase).T).astype(ml_dtypes.bfloat16)
    back[LANES : LANES + half] = (-scaled * np.sin(phase).T).astype(ml_dtypes.bfloat16)
    order = (np.arange(count)[None, :] * group + np.arange(group)[:, None]).reshape(-1)
    left_t = np.zeros((2 * pad, side), ml_dtypes.bfloat16)
    left_t[:half] = cos.T
    left_t[pad : pad + half] = sin.T
    left_m = left_t[:, order]
    left_i = left_m.T.copy()
    right_m = np.zeros((group, 2 * LANES, 2 * LANES), ml_dtypes.bfloat16)
    back_m = np.zeros((group, 2 * LANES, 2 * LANES), ml_dtypes.bfloat16)
    for r in range(group):
        at = side * r - LANES * r
        right_m[r, at : at + side] = right
        back_m[r, :, at : at + side] = back
    power = np.zeros((2, pad, LANES), np.float32)
    power[:, :half, :half] = counts[None, None, :]
    power[1, 0] = 0.0
    power[1, side // 2] = 0.0
    return right, right_m, left_t, left_m, left_i, back_m, power


def mm(a, b):
    return jnp.dot(a, b, preferred_element_type=jnp.float32)


def halves(left, segment, pad):
    both = mm(left, segment)
    p_re, p_im = both[:pad, :LANES], both[:pad, LANES:]
    q_re, q_im = both[pad:, :LANES], both[pad:, LANES:]
    return [x.astype(jnp.bfloat16) for x in (p_re + q_im, p_im - q_re, p_re - q_im, p_im + q_re)]


def flipped(place, step, bits):
    total = 0
    for b in range(bits):
        total = total + (place // (1 << b) + step // (1 << b)) % 2 * (1 << b)
    return total


def exchange(side, peers, layers, cap, chunks_all, group, count, pad,
             packed, ints, steps, shard, right_m, left_m,
             spec, anchor, ints_out, steps_out,
             landed, pix, blk_send, blk_recv, int_send, int_recv,
             up_send, up_recv, down_send, down_recv, off_send, off_recv, own_sem):
    bf16 = jnp.bfloat16
    layer, me = lax.axis_index("sec"), lax.axis_index("tile")
    bits = peers.bit_length() - 1
    chunks = group + 1
    barrier = pltpu.get_barrier_semaphore()
    for d in range(1, peers):
        pl.semaphore_signal(barrier, inc=1, device_id=(layer, flipped(me, d, bits)), device_id_type=MESH)
    for d in range(1, layers):
        pl.semaphore_signal(barrier, inc=1, device_id=((layer + d) % layers, me), device_id_type=MESH)
    pl.semaphore_wait(barrier, peers + layers - 2)

    def relay(up, k):
        which = layer - k if up else layer + k
        which = jnp.clip(which, 0, layers - 1)
        return pltpu.make_async_remote_copy(
            src_ref=shard if k == 0 else anchor.at[which],
            dst_ref=anchor.at[which],
            send_sem=(up_send if up else down_send).at[k],
            recv_sem=(up_recv if up else down_recv).at[k],
            device_id=((layer + 1) % layers if up else (layer + layers - 1) % layers, me),
            device_id_type=MESH,
        )

    def sends(up, k):
        return (layer < layers - 1) & (layer >= k) if up else (layer > 0) & (layer + k <= layers - 1)

    def gets(up, k):
        return (layer - 1 >= k) if up else (layer + 1 + k <= layers - 1)

    def start_relay(k):
        for up in (True, False):
            @pl.when(sends(up, k))
            def _():
                relay(up, k).start()

    def block(d):
        other = flipped(me, d, bits)
        return pltpu.make_async_remote_copy(
            src_ref=packed.at[other], dst_ref=landed.at[me],
            send_sem=blk_send.at[d - 1], recv_sem=blk_recv.at[d - 1],
            device_id=(layer, other), device_id_type=MESH,
        )

    def small(d):
        other = flipped(me, d, bits)
        return pltpu.make_async_remote_copy(
            src_ref=ints.at[other], dst_ref=ints_out.at[me],
            send_sem=int_send.at[d - 1], recv_sem=int_recv.at[d - 1],
            device_id=(layer, other), device_id_type=MESH,
        )

    def offset(d):
        return pltpu.make_async_remote_copy(
            src_ref=steps, dst_ref=steps_out.at[layer],
            send_sem=off_send.at[d - 1], recv_sem=off_recv.at[d - 1],
            device_id=((layer + d) % layers, me), device_id_type=MESH,
        )

    start_relay(0)
    for d in range(1, peers):
        block(d).start()
    for d in range(1, peers):
        small(d).start()
    for d in range(1, layers):
        offset(d).start()
    own = [
        pltpu.make_async_copy(packed.at[me], landed.at[me], own_sem.at[0]),
        pltpu.make_async_copy(ints.at[me], ints_out.at[me], own_sem.at[1]),
        pltpu.make_async_copy(steps, steps_out.at[layer], own_sem.at[2]),
        pltpu.make_async_copy(shard, anchor.at[layer], own_sem.at[3]),
    ]
    for x in own:
        x.start()
    own[0].wait()

    some = min(BATCH, cap)

    def process(d, carry):
        source = flipped(me, d, bits)

        def spread(i, inner):
            for u in range(8):
                t = i * 8 + u
                at = pl.multiple_of(t * LANES, LANES)
                pix[pl.ds(t, cap, stride=chunks_all), :] = landed[source, :, pl.ds(at, LANES)].astype(jnp.float32)
            return inner

        lax.fori_loop(0, chunks_all // 8, spread, 0)
        for first in range(0, cap, some):
            pieces = [
                [pix[pl.ds((first + u) * chunks_all + q, count, stride=chunks), :] for q in range(chunks)]
                for u in range(some)
            ]
            seg = []
            for r in range(group):
                lhs = jnp.concatenate(
                    [jnp.concatenate([x[r], x[r + 1]], axis=1) for x in pieces], axis=0
                ).astype(bf16)
                seg.append(mm(lhs, right_m[r]))
            for u in range(some):
                one = jnp.concatenate([x[u * count : (u + 1) * count] for x in seg], axis=0).astype(bf16)
                for h, part in enumerate(halves(left_m[...], one, pad)):
                    spec[source * cap + first + u, h] = part
        return carry

    def step(d, carry):
        block(d).wait_recv()
        return process(d, carry)

    process(0, 0)
    cuts = [1 + (peers - 1) * i // (layers - 1) for i in range(layers)]
    for k in range(layers - 1):
        lax.fori_loop(cuts[k], cuts[k + 1], step, 0)
        for up in (True, False):
            @pl.when(gets(up, k))
            def _():
                relay(up, k).wait_recv()
        if k < layers - 2:
            start_relay(k + 1)
    for k in range(layers - 1):
        for up in (True, False):
            @pl.when(sends(up, k))
            def _():
                relay(up, k).wait_send()
    for d in range(1, peers):
        block(d).wait_send()
        small(d).wait()
    for d in range(1, layers):
        offset(d).wait()
    for x in own[1:]:
        x.wait()


def correlate(side, slots, cap, layers, chunks_all, group, count, pad, ints, steps, spec, anchor_in, right,
              left_t, left_i, back_m, power, out, pix, anchor, todo):
    chunks = group + 1
    f32, bf16 = jnp.float32, jnp.bfloat16
    rows_in, width = anchor_in.shape
    layer = lax.axis_index("sec")
    tall = ints.shape[0] * cap // slots
    drift = [sum(jnp.where(z <= layer, steps[z * steps.shape[0] // layers, a], 0) for z in range(layers)) for a in (0, 1)]

    def widen(i, carry):
        at = pl.multiple_of(i * 32, 32)
        for c in range(width // LANES):
            wide = anchor_in[pl.ds(at, 32), c * LANES : (c + 1) * LANES].astype(f32)
            anchor[pl.ds(at + c * rows_in, 32), :] = wide
        return carry

    lax.fori_loop(0, rows_in // 32, widen, 0)

    def root(i, a):
        return ints[i // cap * tall + lax.rem(i, cap), a]

    def listed(i, used):
        todo[used] = i
        held = root(i, 0) > 0

        @pl.when(jnp.logical_not(held))
        def _():
            pix[pl.ds(i * chunks_all, chunks_all), :] = jnp.zeros((chunks_all, LANES), f32)

        return used + held.astype(jnp.int32)

    used = lax.fori_loop(0, slots, listed, jnp.int32(0))
    for u in range(BATCH):
        todo[used + u] = slots

    lane = lax.broadcasted_iota(jnp.int32, (side, LANES), 1)
    at_row = lax.broadcasted_iota(jnp.int32, (pad, LANES), 0)
    edge = (at_row != 0) & (at_row != side // 2)

    def window(here):
        row = jnp.clip(root(here, 0) + drift[0], 0, rows_in - side)
        col = jnp.clip(root(here, 1) + drift[1], 0, width - side)
        chunk = col // LANES
        off = col - chunk * LANES
        turn = lax.rem(LANES - off, LANES)
        pieces = []
        for u in range(3):
            at = jnp.minimum(chunk + u, width // LANES - 1) * rows_in + row
            pieces.append(pltpu.roll(anchor[pl.ds(at, side), :], turn, 1))
        keep = lane < LANES - off
        first = jnp.where(keep, pieces[0], pieces[1])
        second = jnp.where(keep, pieces[1], pieces[2])
        return jnp.concatenate([first, second], axis=1)[:, :side].astype(bf16)

    def batch(i, carry):
        ids = [todo[i * BATCH + u] for u in range(BATCH)]
        safe = [jnp.minimum(s, slots - 1) for s in ids]
        wins = jnp.concatenate([window(s) for s in safe], axis=0)
        seg_t = mm(wins, right[...]).astype(bf16)
        turned = []
        for u in range(BATCH):
            move = [spec[safe[u], h].astype(f32) for h in range(4)]
            tmpl = [x.astype(f32) for x in halves(left_t[...], seg_t[u * side : (u + 1) * side], pad)]
            energy, cross = [], []
            for h in range(2):
                a_re, a_im = move[2 * h], move[2 * h + 1]
                b_re, b_im = tmpl[2 * h], tmpl[2 * h + 1]
                cross.append((a_re * b_re + a_im * b_im, a_im * b_re - a_re * b_im))
                energy.append(0.5 * (a_re * a_re + a_im * a_im + b_re * b_re + b_im * b_im))
            total = jnp.sum(energy[0] * power[0] + energy[1] * power[1])
            floor = 0.1 * (total / (side * side)) + 1e-05
            white = []
            for h in range(2):
                inverse = 1.0 / (energy[h] + floor)
                pair = [(x * inverse).astype(bf16).astype(f32) for x in cross[h]]
                if h == 1:
                    pair = [jnp.where(edge, x, 0.0) for x in pair]
                white.append(pair)
            (p_re, p_im), (m_re, m_im) = white
            rhs = jnp.concatenate(
                [
                    jnp.concatenate([p_re + m_re, p_im + m_im], axis=1),
                    jnp.concatenate([m_im - p_im, p_re - m_re], axis=1),
                ],
                axis=0,
            ).astype(bf16)
            turned.append(mm(left_i[...], rhs))
        prior = None
        for r in range(group):
            lhs = jnp.concatenate([x[r * count : (r + 1) * count] for x in turned], axis=0).astype(bf16)
            got = mm(lhs, back_m[r])
            now = got[:, :LANES] if prior is None else prior + got[:, :LANES]
            for u, s in enumerate(ids):
                pix[pl.ds(s * chunks_all + r, count, stride=chunks), :] = now[u * count : (u + 1) * count]
            prior = got[:, LANES:]
        for u, s in enumerate(ids):
            pix[pl.ds(s * chunks_all + group, count, stride=chunks), :] = prior[u * count : (u + 1) * count]
        return carry

    lax.fori_loop(0, (used + BATCH - 1) // BATCH, batch, 0)

    def gather(i, carry):
        for u in range(8):
            t = i * 8 + u
            at = pl.multiple_of(t * LANES, LANES)
            for g in range(slots // 16):
                low = pix[pl.ds(g * 16 * chunks_all + t, 8, stride=chunks_all), :]
                high = pix[pl.ds((g * 16 + 8) * chunks_all + t, 8, stride=chunks_all), :]
                out[g * 16 : g * 16 + 16, pl.ds(at, LANES)] = jnp.concatenate([low, high], axis=0).astype(bf16)
        return carry

    lax.fori_loop(0, chunks_all // 8, gather, 0)


def sharpened(packed, ints, steps, shard, layers):
    peers, cap, area = packed.shape
    slots = peers * cap
    side = math.isqrt(area)
    right, right_m, left_t, left_m, left_i, back_m, power = [jnp.asarray(x) for x in tables(side)]
    group, pad = right_m.shape[0], power.shape[1]
    count, chunks_all = side // group, area // LANES
    rows, width = shard.shape
    vmem = pl.BlockSpec(memory_space=pltpu.VMEM)
    smem = pl.BlockSpec(memory_space=pltpu.SMEM)
    hbm = pl.BlockSpec(memory_space=pl.ANY)
    dma = pltpu.SemaphoreType.DMA
    spec, anchor, ints_all, steps_all = pl.pallas_call(
        functools.partial(exchange, side, peers, layers, cap, chunks_all, group, count, pad),
        out_shape=[
            jax.ShapeDtypeStruct((slots, 4, pad, LANES), jnp.bfloat16),
            jax.ShapeDtypeStruct((layers, rows, width), shard.dtype),
            jax.ShapeDtypeStruct(ints.shape, ints.dtype),
            jax.ShapeDtypeStruct((layers,) + steps.shape, steps.dtype),
        ],
        in_specs=[vmem, hbm, hbm, hbm, vmem, vmem],
        out_specs=[vmem, hbm, hbm, hbm],
        scratch_shapes=[
            pltpu.VMEM(packed.shape, packed.dtype),
            pltpu.VMEM((cap * chunks_all, LANES), jnp.float32),
            dma((peers - 1,)), dma((peers - 1,)), dma((peers - 1,)), dma((peers - 1,)),
            dma((layers - 1,)), dma((layers - 1,)), dma((layers - 1,)), dma((layers - 1,)),
            dma((layers - 1,)), dma((layers - 1,)), dma((4,)),
        ],
        compiler_params=pltpu.CompilerParams(vmem_limit_bytes=48 << 20, collective_id=0, has_side_effects=True),
        name="exchange",
    )(packed, ints, steps, shard, right_m, left_m)
    return pl.pallas_call(
        functools.partial(correlate, side, slots, cap, layers, chunks_all, group, count, pad),
        out_shape=jax.ShapeDtypeStruct((slots, area), jnp.bfloat16),
        in_specs=[smem, smem] + [vmem] * 7,
        out_specs=vmem,
        scratch_shapes=[
            pltpu.VMEM(((slots + 1) * chunks_all, LANES), jnp.float32),
            pltpu.VMEM((layers * rows * width // LANES, LANES), jnp.float32),
            pltpu.SMEM((slots + BATCH + 1,), jnp.int32),
        ],
        compiler_params=pltpu.CompilerParams(vmem_limit_bytes=48 << 20),
        name="correlate",
    )(
        ints_all.reshape(-1, LANES), steps_all.reshape(-1, LANES), spec,
        anchor.reshape(layers * rows, width), right, left_t, left_i, back_m, power,
    )


def slot_ranks(target):
    positions = jnp.arange(target.shape[0], dtype=jnp.int32)
    earlier = (target[:, None] == target[None, :]) & (positions[None, :] < positions[:, None])
    return jnp.sum(earlier.astype(jnp.int32), axis=1)


def body(rendered, cached, owners, roots, offsets):
    area = cached.shape[2]
    held = cached.shape[1]
    owner_count = lax.axis_size("tile")
    capacity = max(2, 2 * held // owner_count)
    target = owners[0, :, 0]
    tall = -(-capacity // 8) * 8
    rank = slot_ranks(target)
    slots_all = jnp.arange(owner_count * capacity, dtype=jnp.int32)
    selector = slots_all[:, None] == (target * capacity + rank)[None, :]
    tall_all = jnp.arange(owner_count * tall, dtype=jnp.int32)
    tall_sel = tall_all[:, None] == (target * tall + rank)[None, :]
    wide = jnp.pad(roots[0], ((0, 0), (0, LANES - 2)))
    ints = jnp.sum(jnp.where(tall_sel[:, :, None], wide[None, :, :], 0), axis=1)
    ints = ints.reshape(owner_count, tall, LANES)
    steps = jnp.pad(offsets, ((0, 7), (0, LANES - 2)))
    packed = jnp.dot(selector.astype(jnp.bfloat16), cached[0], preferred_element_type=jnp.float32)
    packed = packed.astype(jnp.bfloat16).reshape(owner_count, capacity, area)
    result = sharpened(packed, ints, steps, rendered[0], lax.axis_size("sec"))
    return result.reshape(1, 1, owner_count, capacity, area)


def solution(mesh):
    placed = (
        P("tile", "sec", None),
        P("sec", "tile", None),
        P("sec", "tile", None),
        P("sec", "tile", None),
        P("sec", None),
    )
    return jax.shard_map(
        body,
        mesh=mesh,
        in_specs=placed,
        out_specs=P("sec", "tile", None, None, None),
        check_vma=False,
    )
```

```python
import functools
import math

import jax
import jax.numpy as jnp
import ml_dtypes
import numpy as np
from jax import lax
from jax.experimental import pallas as pl
from jax.experimental.pallas import tpu as pltpu
from jax.sharding import PartitionSpec as P

LANES = 128
BATCH = 8
MESH = pl.DeviceIdType.MESH


def tables(side):
    half = side // 2 + 1
    pad = -(-half // 8) * 8
    group = side // 32 - 1
    count = side // group
    full = np.arange(side)
    low = np.arange(half)
    phase = (full[:, None] * low[None, :] % side).astype(np.float32) * np.float32(2.0 * math.pi / side)
    cos = np.cos(phase).astype(ml_dtypes.bfloat16)
    sin = np.sin(phase).astype(ml_dtypes.bfloat16)
    counts = np.where((low == 0) | (low == side // 2), 1.0, 2.0).astype(np.float32)
    right = np.zeros((side, 2 * LANES), ml_dtypes.bfloat16)
    right[:, :half] = cos
    right[:, LANES : LANES + half] = -sin
    back = np.zeros((2 * LANES, side), ml_dtypes.bfloat16)
    scaled = counts[:, None] / np.float32(side)
    back[:half] = (scaled * np.cos(phase).T).astype(ml_dtypes.bfloat16)
    back[LANES : LANES + half] = (-scaled * np.sin(phase).T).astype(ml_dtypes.bfloat16)
    order = (np.arange(count)[None, :] * group + np.arange(group)[:, None]).reshape(-1)
    left_t = np.zeros((2 * pad, side), ml_dtypes.bfloat16)
    left_t[:half] = cos.T
    left_t[pad : pad + half] = sin.T
    left_m = left_t[:, order]
    left_i = left_m.T.copy()
    right_m = np.zeros((group, 2 * LANES, 2 * LANES), ml_dtypes.bfloat16)
    back_m = np.zeros((group, 2 * LANES, 2 * LANES), ml_dtypes.bfloat16)
    for r in range(group):
        at = side * r - LANES * r
        right_m[r, at : at + side] = right
        back_m[r, :, at : at + side] = back
    power = np.zeros((2, pad, LANES), np.float32)
    power[:, :half, :half] = counts[None, None, :]
    power[1, 0] = 0.0
    power[1, side // 2] = 0.0
    return right, right_m, left_t, left_m, left_i, back_m, power


def mm(a, b):
    return jnp.dot(a, b, preferred_element_type=jnp.float32)


def halves(left, segment, pad, kind=jnp.bfloat16):
    both = mm(left, segment)
    p_re, p_im = both[:pad, :LANES], both[:pad, LANES:]
    q_re, q_im = both[pad:, :LANES], both[pad:, LANES:]
    return [x.astype(kind) for x in (p_re + q_im, p_im - q_re, p_re - q_im, p_im + q_re)]


def flipped(place, step, bits):
    total = 0
    for b in range(bits):
        total = total + (place // (1 << b) + step // (1 << b)) % 2 * (1 << b)
    return total


def exchange(side, peers, layers, cap, chunks_all, group, count, pad,
             packed, ints, steps, shard, right_m, left_m,
             spec, anchor, ints_out, steps_out,
             landed, pix, made, made_sem, blk_send, blk_recv, int_send, int_recv,
             up_send, up_recv, down_send, down_recv, off_send, off_recv, own_sem):
    bf16 = jnp.bfloat16
    layer, me = lax.axis_index("sec"), lax.axis_index("tile")
    bits = peers.bit_length() - 1
    chunks = group + 1
    barrier = pltpu.get_barrier_semaphore()
    for d in range(1, peers):
        pl.semaphore_signal(barrier, inc=1, device_id=(layer, flipped(me, d, bits)), device_id_type=MESH)
    for d in range(1, layers):
        pl.semaphore_signal(barrier, inc=1, device_id=((layer + d) % layers, me), device_id_type=MESH)
    pl.semaphore_wait(barrier, peers + layers - 2)

    def relay(up, k):
        which = layer - k if up else layer + k
        which = jnp.clip(which, 0, layers - 1)
        return pltpu.make_async_remote_copy(
            src_ref=shard if k == 0 else anchor.at[which],
            dst_ref=anchor.at[which],
            send_sem=(up_send if up else down_send).at[k],
            recv_sem=(up_recv if up else down_recv).at[k],
            device_id=((layer + 1) % layers if up else (layer + layers - 1) % layers, me),
            device_id_type=MESH,
        )

    def sends(up, k):
        return (layer < layers - 1) & (layer >= k) if up else (layer > 0) & (layer + k <= layers - 1)

    def gets(up, k):
        return (layer - 1 >= k) if up else (layer + 1 + k <= layers - 1)

    def start_relay(k):
        for up in (True, False):
            @pl.when(sends(up, k))
            def _():
                relay(up, k).start()

    def block(d):
        other = flipped(me, d, bits)
        return pltpu.make_async_remote_copy(
            src_ref=packed.at[other], dst_ref=landed.at[me],
            send_sem=blk_send.at[d - 1], recv_sem=blk_recv.at[d - 1],
            device_id=(layer, other), device_id_type=MESH,
        )

    def small(d):
        other = flipped(me, d, bits)
        return pltpu.make_async_remote_copy(
            src_ref=ints.at[other], dst_ref=ints_out.at[me],
            send_sem=int_send.at[d - 1], recv_sem=int_recv.at[d - 1],
            device_id=(layer, other), device_id_type=MESH,
        )

    def offset(d):
        return pltpu.make_async_remote_copy(
            src_ref=steps, dst_ref=steps_out.at[layer],
            send_sem=off_send.at[d - 1], recv_sem=off_recv.at[d - 1],
            device_id=((layer + d) % layers, me), device_id_type=MESH,
        )

    start_relay(0)
    for d in range(1, peers):
        block(d).start()
    for d in range(1, peers):
        small(d).start()
    for d in range(1, layers):
        offset(d).start()
    own = [
        pltpu.make_async_copy(packed.at[me], landed.at[me], own_sem.at[0]),
        pltpu.make_async_copy(ints.at[me], ints_out.at[me], own_sem.at[1]),
        pltpu.make_async_copy(steps, steps_out.at[layer], own_sem.at[2]),
        pltpu.make_async_copy(shard, anchor.at[layer], own_sem.at[3]),
    ]
    for x in own:
        x.start()
    own[0].wait()

    some = min(BATCH, cap)

    def put(d):
        mine = pl.ds(flipped(me, d, bits) * cap, cap)
        return pltpu.make_async_copy(made.at[mine], spec.at[mine], made_sem.at[d])

    def process(d, carry):
        source = flipped(me, d, bits)

        def spread(i, inner):
            for u in range(8):
                t = i * 8 + u
                at = pl.multiple_of(t * LANES, LANES)
                pix[pl.ds(t, cap, stride=chunks_all), :] = landed[source, :, pl.ds(at, LANES)].astype(jnp.float32)
            return inner

        lax.fori_loop(0, chunks_all // 8, spread, 0)
        for first in range(0, cap, some):
            pieces = [
                [pix[pl.ds((first + u) * chunks_all + q, count, stride=chunks), :] for q in range(chunks)]
                for u in range(some)
            ]
            seg = []
            for r in range(group):
                lhs = jnp.concatenate(
                    [jnp.concatenate([x[r], x[r + 1]], axis=1) for x in pieces], axis=0
                ).astype(bf16)
                seg.append(mm(lhs, right_m[r]))
            for u in range(some):
                one = jnp.concatenate([x[u * count : (u + 1) * count] for x in seg], axis=0).astype(bf16)
                for h, part in enumerate(halves(left_m[...], one, pad)):
                    made[source * cap + first + u, h] = part
        put(d).start()
        return carry

    def step(d, carry):
        block(d).wait_recv()
        return process(d, carry)

    process(0, 0)
    cuts = [1 + (peers - 1) * i // (layers - 1) for i in range(layers)]
    for k in range(layers - 1):
        lax.fori_loop(cuts[k], cuts[k + 1], step, 0)
        for up in (True, False):
            @pl.when(gets(up, k))
            def _():
                relay(up, k).wait_recv()
        if k < layers - 2:
            start_relay(k + 1)
    for k in range(layers - 1):
        for up in (True, False):
            @pl.when(sends(up, k))
            def _():
                relay(up, k).wait_send()
    for d in range(1, peers):
        block(d).wait_send()
        small(d).wait()
    for d in range(1, layers):
        offset(d).wait()
    for x in own[1:]:
        x.wait()
    for d in range(peers):
        put(d).wait()


def correlate(side, slots, cap, layers, chunks_all, group, count, pad, ints, steps, spec_in, anchor_in, right,
              left_t, left_i, back_m, power, out, pix, anchor, ahead, spec, flat, todo, rest, in_sem, out_sem):
    chunks = group + 1
    f32, bf16 = jnp.float32, jnp.bfloat16
    rows_in, width = anchor_in.shape
    fetch = pltpu.make_async_copy(spec_in, spec, in_sem)
    fetch.start()
    layer = lax.axis_index("sec")
    tall = ints.shape[0] * cap // slots
    drift = [sum(jnp.where(z <= layer, steps[z * steps.shape[0] // layers, a], 0) for z in range(layers)) for a in (0, 1)]

    def widen(i, carry):
        at = pl.multiple_of(i * 32, 32)
        for c in range(width // LANES):
            wide = anchor_in[pl.ds(at, 32), c * LANES : (c + 1) * LANES].astype(f32)
            anchor[pl.ds(at + c * rows_in, 32), :] = wide
        return carry

    lax.fori_loop(0, rows_in // 32, widen, 0)

    def root(i, a):
        return ints[i // cap * tall + lax.rem(i, cap), a]

    def listed(i, used):
        for u in range(8):
            here = i * 8 + u
            todo[used] = here
            rest[here - used] = here
            used = used + (root(here, 0) > 0).astype(jnp.int32)
        return used

    used = lax.fori_loop(0, slots // 8, listed, jnp.int32(0))

    def clear(i, carry):
        pix[pl.ds(rest[i] * chunks_all, chunks_all), :] = jnp.zeros((chunks_all, LANES), f32)
        return carry

    lax.fori_loop(0, slots - used, clear, 0)
    for u in range(2 * BATCH):
        todo[used + u] = slots

    lane = lax.broadcasted_iota(jnp.int32, (side, LANES), 1)
    at_row = lax.broadcasted_iota(jnp.int32, (pad, LANES), 0)
    edge = (at_row != 0) & (at_row != side // 2)

    def window(here):
        row = jnp.clip(root(here, 0) + drift[0], 0, rows_in - side)
        col = jnp.clip(root(here, 1) + drift[1], 0, width - side)
        chunk = col // LANES
        off = col - chunk * LANES
        turn = lax.rem(LANES - off, LANES)
        pieces = []
        for u in range(3):
            at = jnp.minimum(chunk + u, width // LANES - 1) * rows_in + row
            pieces.append(pltpu.roll(anchor[pl.ds(at, side), :], turn, 1))
        keep = lane < LANES - off
        first = jnp.where(keep, pieces[0], pieces[1])
        second = jnp.where(keep, pieces[1], pieces[2])
        return jnp.concatenate([first, second], axis=1)[:, :side].astype(bf16)

    def front(i):
        safe = [jnp.minimum(todo[i * BATCH + u], slots - 1) for u in range(BATCH)]
        wins = jnp.concatenate([window(s) for s in safe], axis=0)
        seg_t = mm(wins, right[...]).astype(bf16)
        return [halves(left_t[...], seg_t[u * side : (u + 1) * side], pad, f32) for u in range(BATCH)]

    def keep(parts):
        for u in range(BATCH):
            for h in range(4):
                ahead[u, h] = parts[u][h]

    def batch(i, carry):
        ids = [todo[i * BATCH + u] for u in range(BATCH)]
        safe = [jnp.minimum(s, slots - 1) for s in ids]
        turned = []
        for u in range(BATCH):
            move = [spec[safe[u], h].astype(f32) for h in range(4)]
            tmpl = [ahead[u, h] for h in range(4)]
            energy, cross = [], []
            for h in range(2):
                a_re, a_im = move[2 * h], move[2 * h + 1]
                b_re, b_im = tmpl[2 * h], tmpl[2 * h + 1]
                cross.append((a_re * b_re + a_im * b_im, a_im * b_re - a_re * b_im))
                energy.append(0.5 * (a_re * a_re + a_im * a_im + b_re * b_re + b_im * b_im))
            total = jnp.sum(energy[0] * power[0] + energy[1] * power[1])
            floor = 0.1 * (total / (side * side)) + 1e-05
            white = []
            for h in range(2):
                inverse = 1.0 / (energy[h] + floor)
                pair = [x * inverse for x in cross[h]]
                if h == 1:
                    pair = [jnp.where(edge, x, 0.0) for x in pair]
                white.append(pair)
            (p_re, p_im), (m_re, m_im) = white
            rhs = jnp.concatenate(
                [
                    jnp.concatenate([p_re + m_re, p_im + m_im], axis=1),
                    jnp.concatenate([m_im - p_im, p_re - m_re], axis=1),
                ],
                axis=0,
            ).astype(bf16)
            turned.append(mm(left_i[...], rhs))
        parts = front(i + 1)
        prior = None
        for r in range(group):
            lhs = jnp.concatenate([x[r * count : (r + 1) * count] for x in turned], axis=0).astype(bf16)
            got = mm(lhs, back_m[r])
            now = got[:, :LANES] if prior is None else prior + got[:, :LANES]
            for u, s in enumerate(ids):
                pix[pl.ds(s * chunks_all + r, count, stride=chunks), :] = now[u * count : (u + 1) * count]
            prior = got[:, LANES:]
        for u, s in enumerate(ids):
            pix[pl.ds(s * chunks_all + group, count, stride=chunks), :] = prior[u * count : (u + 1) * count]
        keep(parts)
        return carry

    keep(front(0))
    fetch.wait()
    lax.fori_loop(0, (used + BATCH - 1) // BATCH, batch, 0)

    def put(g):
        mine = pl.ds(g * 16, 16)
        return pltpu.make_async_copy(flat.at[mine], out.at[mine], out_sem.at[g])

    for g in range(slots // 16):

        def gather(i, carry):
            for u in range(20):
                t = i * 20 + u
                at = pl.multiple_of(t * LANES, LANES)
                low = pix[pl.ds(g * 16 * chunks_all + t, 8, stride=chunks_all), :]
                high = pix[pl.ds((g * 16 + 8) * chunks_all + t, 8, stride=chunks_all), :]
                flat[g * 16 : g * 16 + 16, pl.ds(at, LANES)] = jnp.concatenate([low, high], axis=0).astype(bf16)
            return carry

        lax.fori_loop(0, chunks_all // 20, gather, 0)
        put(g).start()
    for g in range(slots // 16):
        put(g).wait()


def sharpened(packed, ints, steps, shard, layers):
    peers, cap, area = packed.shape
    slots = peers * cap
    side = math.isqrt(area)
    right, right_m, left_t, left_m, left_i, back_m, power = [jnp.asarray(x) for x in tables(side)]
    group, pad = right_m.shape[0], power.shape[1]
    count, chunks_all = side // group, area // LANES
    rows, width = shard.shape
    vmem = pl.BlockSpec(memory_space=pltpu.VMEM)
    smem = pl.BlockSpec(memory_space=pltpu.SMEM)
    hbm = pl.BlockSpec(memory_space=pl.ANY)
    dma = pltpu.SemaphoreType.DMA
    spec, anchor, ints_all, steps_all = pl.pallas_call(
        functools.partial(exchange, side, peers, layers, cap, chunks_all, group, count, pad),
        out_shape=[
            jax.ShapeDtypeStruct((slots, 4, pad, LANES), jnp.bfloat16),
            jax.ShapeDtypeStruct((layers, rows, width), shard.dtype),
            jax.ShapeDtypeStruct(ints.shape, ints.dtype),
            jax.ShapeDtypeStruct((layers,) + steps.shape, steps.dtype),
        ],
        in_specs=[vmem, hbm, hbm, hbm, vmem, vmem],
        out_specs=[hbm] * 4,
        scratch_shapes=[
            pltpu.VMEM(packed.shape, packed.dtype),
            pltpu.VMEM((cap * chunks_all, LANES), jnp.float32),
            pltpu.VMEM((slots, 4, pad, LANES), jnp.bfloat16),
            dma((peers,)),
            dma((peers - 1,)), dma((peers - 1,)), dma((peers - 1,)), dma((peers - 1,)),
            dma((layers - 1,)), dma((layers - 1,)), dma((layers - 1,)), dma((layers - 1,)),
            dma((layers - 1,)), dma((layers - 1,)), dma((4,)),
        ],
        compiler_params=pltpu.CompilerParams(vmem_limit_bytes=48 << 20, collective_id=0, has_side_effects=True),
        name="exchange",
    )(packed, ints, steps, shard, right_m, left_m)
    return pl.pallas_call(
        functools.partial(correlate, side, slots, cap, layers, chunks_all, group, count, pad),
        out_shape=jax.ShapeDtypeStruct((slots, area), jnp.bfloat16),
        in_specs=[smem, smem, hbm] + [vmem] * 6,
        out_specs=hbm,
        scratch_shapes=[
            pltpu.VMEM(((slots + 1) * chunks_all, LANES), jnp.float32),
            pltpu.VMEM((layers * rows * width // LANES, LANES), jnp.float32),
            pltpu.VMEM((BATCH, 4, pad, LANES), jnp.float32),
            pltpu.VMEM((slots, 4, pad, LANES), jnp.bfloat16),
            pltpu.VMEM((slots, area), jnp.bfloat16),
            pltpu.SMEM((slots + 2 * BATCH + 1,), jnp.int32),
            pltpu.SMEM((slots + 1,), jnp.int32),
            dma(()),
            dma((slots // 16,)),
        ],
        compiler_params=pltpu.CompilerParams(vmem_limit_bytes=48 << 20),
        name="correlate",
    )(
        ints_all.reshape(-1, LANES), steps_all.reshape(-1, LANES), spec,
        anchor.reshape(layers * rows, width), right, left_t, left_i, back_m, power,
    )


def slot_ranks(target):
    positions = jnp.arange(target.shape[0], dtype=jnp.int32)
    earlier = (target[:, None] == target[None, :]) & (positions[None, :] < positions[:, None])
    return jnp.sum(earlier.astype(jnp.int32), axis=1)


def body(rendered, cached, owners, roots, offsets):
    area = cached.shape[2]
    held = cached.shape[1]
    owner_count = lax.axis_size("tile")
    capacity = max(2, 2 * held // owner_count)
    target = owners[0, :, 0]
    tall = -(-capacity // 8) * 8
    rank = slot_ranks(target)
    slots_all = jnp.arange(owner_count * capacity, dtype=jnp.int32)
    selector = slots_all[:, None] == (target * capacity + rank)[None, :]
    tall_all = jnp.arange(owner_count * tall, dtype=jnp.int32)
    tall_sel = tall_all[:, None] == (target * tall + rank)[None, :]
    wide = jnp.pad(roots[0], ((0, 0), (0, LANES - 2)))
    ints = jnp.sum(jnp.where(tall_sel[:, :, None], wide[None, :, :], 0), axis=1)
    ints = ints.reshape(owner_count, tall, LANES)
    steps = jnp.pad(offsets, ((0, 7), (0, LANES - 2)))
    packed = jnp.dot(selector.astype(jnp.bfloat16), cached[0], preferred_element_type=jnp.float32)
    packed = packed.astype(jnp.bfloat16).reshape(owner_count, capacity, area)
    result = sharpened(packed, ints, steps, rendered[0], lax.axis_size("sec"))
    return result.reshape(1, 1, owner_count, capacity, area)


def solution(mesh):
    placed = (
        P("tile", "sec", None),
        P("sec", "tile", None),
        P("sec", "tile", None),
        P("sec", "tile", None),
        P("sec", None),
    )
    return jax.shard_map(
        body,
        mesh=mesh,
        in_specs=placed,
        out_specs=P("sec", "tile", None, None, None),
        check_vma=False,
    )
```

```python
import functools
import math

import jax
import jax.numpy as jnp
import ml_dtypes
import numpy as np
from jax import lax
from jax.experimental import pallas as pl
from jax.experimental.pallas import tpu as pltpu
from jax.sharding import PartitionSpec as P

LANES = 128
BATCH = 8
MESH = pl.DeviceIdType.MESH


def tables(side):
    half = side // 2 + 1
    pad = -(-half // 8) * 8
    group = side // 32 - 1
    count = side // group
    full = np.arange(side)
    low = np.arange(half)
    phase = (full[:, None] * low[None, :] % side).astype(np.float32) * np.float32(2.0 * math.pi / side)
    cos = np.cos(phase).astype(ml_dtypes.bfloat16)
    sin = np.sin(phase).astype(ml_dtypes.bfloat16)
    counts = np.where((low == 0) | (low == side // 2), 1.0, 2.0).astype(np.float32)
    right = np.zeros((side, 2 * LANES), ml_dtypes.bfloat16)
    right[:, :half] = cos
    right[:, LANES : LANES + half] = -sin
    back = np.zeros((2 * LANES, side), ml_dtypes.bfloat16)
    scaled = counts[:, None] / np.float32(side)
    back[:half] = (scaled * np.cos(phase).T).astype(ml_dtypes.bfloat16)
    back[LANES : LANES + half] = (-scaled * np.sin(phase).T).astype(ml_dtypes.bfloat16)
    order = (np.arange(count)[None, :] * group + np.arange(group)[:, None]).reshape(-1)
    left_t = np.zeros((2 * pad, side), ml_dtypes.bfloat16)
    left_t[:half] = cos.T
    left_t[pad : pad + half] = sin.T
    left_m = left_t[:, order]
    left_i = left_m.T.copy()
    right_m = np.zeros((group, 2 * LANES, 2 * LANES), ml_dtypes.bfloat16)
    back_m = np.zeros((group, 2 * LANES, 2 * LANES), ml_dtypes.bfloat16)
    for r in range(group):
        at = side * r - LANES * r
        right_m[r, at : at + side] = right
        back_m[r, :, at : at + side] = back
    power = np.zeros((2, pad, LANES), np.float32)
    power[:, :half, :half] = counts[None, None, :]
    power[1, 0] = 0.0
    power[1, side // 2] = 0.0
    return right, right_m, left_t, left_m, left_i, back_m, power


def mm(a, b):
    return jnp.dot(a, b, preferred_element_type=jnp.float32)


def halves(left, segment, pad, kind=jnp.bfloat16):
    both = mm(left, segment)
    p_re, p_im = both[:pad, :LANES], both[:pad, LANES:]
    q_re, q_im = both[pad:, :LANES], both[pad:, LANES:]
    return [x.astype(kind) for x in (p_re + q_im, p_im - q_re, p_re - q_im, p_im + q_re)]


def flipped(place, step, bits):
    total = 0
    for b in range(bits):
        total = total + (place // (1 << b) + step // (1 << b)) % 2 * (1 << b)
    return total


def exchange(side, peers, layers, cap, chunks_all, group, count, pad,
             packed, ints, steps, shard, right_m, left_m,
             spec, anchor, ints_out, steps_out,
             landed, pix, made, made_sem, blk_send, blk_recv, int_send, int_recv,
             up_send, up_recv, down_send, down_recv, off_send, off_recv, own_sem):
    bf16 = jnp.bfloat16
    layer, me = lax.axis_index("sec"), lax.axis_index("tile")
    bits = peers.bit_length() - 1
    chunks = group + 1
    barrier = pltpu.get_barrier_semaphore()
    for d in range(1, peers):
        pl.semaphore_signal(barrier, inc=1, device_id=(layer, flipped(me, d, bits)), device_id_type=MESH)
    for d in range(1, layers):
        pl.semaphore_signal(barrier, inc=1, device_id=((layer + d) % layers, me), device_id_type=MESH)
    pl.semaphore_wait(barrier, peers + layers - 2)

    def relay(up, k):
        which = layer - k if up else layer + k
        which = jnp.clip(which, 0, layers - 1)
        return pltpu.make_async_remote_copy(
            src_ref=shard if k == 0 else anchor.at[which],
            dst_ref=anchor.at[which],
            send_sem=(up_send if up else down_send).at[k],
            recv_sem=(up_recv if up else down_recv).at[k],
            device_id=((layer + 1) % layers if up else (layer + layers - 1) % layers, me),
            device_id_type=MESH,
        )

    def sends(up, k):
        return (layer < layers - 1) & (layer >= k) if up else (layer > 0) & (layer + k <= layers - 1)

    def gets(up, k):
        return (layer - 1 >= k) if up else (layer + 1 + k <= layers - 1)

    def start_relay(k):
        for up in (True, False):
            @pl.when(sends(up, k))
            def _():
                relay(up, k).start()

    def block(d):
        other = flipped(me, d, bits)
        return pltpu.make_async_remote_copy(
            src_ref=packed.at[other], dst_ref=landed.at[me],
            send_sem=blk_send.at[d - 1], recv_sem=blk_recv.at[d - 1],
            device_id=(layer, other), device_id_type=MESH,
        )

    def small(d):
        other = flipped(me, d, bits)
        return pltpu.make_async_remote_copy(
            src_ref=ints.at[other], dst_ref=ints_out.at[me],
            send_sem=int_send.at[d - 1], recv_sem=int_recv.at[d - 1],
            device_id=(layer, other), device_id_type=MESH,
        )

    def offset(d):
        return pltpu.make_async_remote_copy(
            src_ref=steps, dst_ref=steps_out.at[layer],
            send_sem=off_send.at[d - 1], recv_sem=off_recv.at[d - 1],
            device_id=((layer + d) % layers, me), device_id_type=MESH,
        )

    start_relay(0)
    for d in range(1, peers):
        block(d).start()
    for d in range(1, peers):
        small(d).start()
    for d in range(1, layers):
        offset(d).start()
    own = [
        pltpu.make_async_copy(packed.at[me], landed.at[me], own_sem.at[0]),
        pltpu.make_async_copy(ints.at[me], ints_out.at[me], own_sem.at[1]),
        pltpu.make_async_copy(steps, steps_out.at[layer], own_sem.at[2]),
        pltpu.make_async_copy(shard, anchor.at[layer], own_sem.at[3]),
    ]
    for x in own:
        x.start()
    own[0].wait()

    some = min(BATCH, cap)

    def put(d):
        mine = pl.ds(flipped(me, d, bits) * cap, cap)
        return pltpu.make_async_copy(made.at[mine], spec.at[mine], made_sem.at[d])

    def process(d, carry):
        source = flipped(me, d, bits)

        def spread(i, inner):
            for u in range(8):
                t = i * 8 + u
                at = pl.multiple_of(t * LANES, LANES)
                pix[pl.ds(t, cap, stride=chunks_all), :] = landed[source, :, pl.ds(at, LANES)].astype(jnp.float32)
            return inner

        lax.fori_loop(0, chunks_all // 8, spread, 0)
        for first in range(0, cap, some):
            pieces = [
                [pix[pl.ds((first + u) * chunks_all + q, count, stride=chunks), :] for q in range(chunks)]
                for u in range(some)
            ]
            seg = []
            for r in range(group):
                lhs = jnp.concatenate(
                    [jnp.concatenate([x[r], x[r + 1]], axis=1) for x in pieces], axis=0
                ).astype(bf16)
                seg.append(mm(lhs, right_m[r]))
            for u in range(some):
                one = jnp.concatenate([x[u * count : (u + 1) * count] for x in seg], axis=0).astype(bf16)
                for h, part in enumerate(halves(left_m[...], one, pad)):
                    made[source * cap + first + u, h] = part
        put(d).start()
        return carry

    def step(d, carry):
        block(d).wait_recv()
        return process(d, carry)

    process(0, 0)
    cuts = [1 + (peers - 1) * i // (layers - 1) for i in range(layers)]
    for k in range(layers - 1):
        lax.fori_loop(cuts[k], cuts[k + 1], step, 0)
        for up in (True, False):
            @pl.when(gets(up, k))
            def _():
                relay(up, k).wait_recv()
        if k < layers - 2:
            start_relay(k + 1)
    for k in range(layers - 1):
        for up in (True, False):
            @pl.when(sends(up, k))
            def _():
                relay(up, k).wait_send()
    for d in range(1, peers):
        block(d).wait_send()
        small(d).wait()
    for d in range(1, layers):
        offset(d).wait()
    for x in own[1:]:
        x.wait()
    for d in range(peers):
        put(d).wait()


def correlate(side, slots, cap, layers, chunks_all, group, count, pad, ints, steps, spec_in, anchor_in, right,
              left_t, left_i, back_m, power, out, pix, anchor, ahead, spec, flat, todo, rest, in_sem, out_sem):
    chunks = group + 1
    f32, bf16 = jnp.float32, jnp.bfloat16
    rows_in, width = anchor_in.shape
    layer = lax.axis_index("sec")
    tall = ints.shape[0] * cap // slots
    drift = [sum(jnp.where(z <= layer, steps[z * steps.shape[0] // layers, a], 0) for z in range(layers)) for a in (0, 1)]

    def widen(i, carry):
        at = pl.multiple_of(i * 32, 32)
        for c in range(width // LANES):
            wide = anchor_in[pl.ds(at, 32), c * LANES : (c + 1) * LANES].astype(f32)
            anchor[pl.ds(at + c * rows_in, 32), :] = wide
        return carry

    lax.fori_loop(0, rows_in // 32, widen, 0)

    def root(i, a):
        return ints[i // cap * tall + lax.rem(i, cap), a]

    def listed(i, used):
        for u in range(8):
            here = i * 8 + u
            todo[used] = here
            rest[here - used] = here
            used = used + (root(here, 0) > 0).astype(jnp.int32)
        return used

    used = lax.fori_loop(0, slots // 8, listed, jnp.int32(0))

    def clear(i, carry):
        pix[pl.ds(rest[i] * chunks_all, chunks_all), :] = jnp.zeros((chunks_all, LANES), f32)
        return carry

    lax.fori_loop(0, slots - used, clear, 0)
    for u in range(2 * BATCH):
        todo[used + u] = slots

    lane = lax.broadcasted_iota(jnp.int32, (side, LANES), 1)
    at_row = lax.broadcasted_iota(jnp.int32, (pad, LANES), 0)
    edge = (at_row != 0) & (at_row != side // 2)

    def window(here):
        row = jnp.clip(root(here, 0) + drift[0], 0, rows_in - side)
        col = jnp.clip(root(here, 1) + drift[1], 0, width - side)
        chunk = col // LANES
        off = col - chunk * LANES
        turn = lax.rem(LANES - off, LANES)
        pieces = []
        for u in range(3):
            at = jnp.minimum(chunk + u, width // LANES - 1) * rows_in + row
            pieces.append(pltpu.roll(anchor[pl.ds(at, side), :], turn, 1))
        keep = lane < LANES - off
        first = jnp.where(keep, pieces[0], pieces[1])
        second = jnp.where(keep, pieces[1], pieces[2])
        return jnp.concatenate([first, second], axis=1)[:, :side].astype(bf16)

    def fetch(i, u):
        place = lax.rem(i, 2)
        slot = jnp.minimum(todo[i * BATCH + u], slots - 1)
        return pltpu.make_async_copy(spec_in.at[slot], spec.at[place, u], in_sem.at[place, u])

    def front(i):
        safe = [jnp.minimum(todo[i * BATCH + u], slots - 1) for u in range(BATCH)]
        wins = jnp.concatenate([window(s) for s in safe], axis=0)
        seg_t = mm(wins, right[...]).astype(bf16)
        return [halves(left_t[...], seg_t[u * side : (u + 1) * side], pad, f32) for u in range(BATCH)]

    def keep(parts):
        for u in range(BATCH):
            for h in range(4):
                ahead[u, h] = parts[u][h]

    def batch(i, carry):
        ids = [todo[i * BATCH + u] for u in range(BATCH)]
        for u in range(BATCH):
            fetch(i + 1, u).start()
        for u in range(BATCH):
            fetch(i, u).wait()
        place = lax.rem(i, 2)
        turned = []
        for u in range(BATCH):
            move = [spec[place, u, h].astype(f32) for h in range(4)]
            tmpl = [ahead[u, h] for h in range(4)]
            energy, cross = [], []
            for h in range(2):
                a_re, a_im = move[2 * h], move[2 * h + 1]
                b_re, b_im = tmpl[2 * h], tmpl[2 * h + 1]
                cross.append((a_re * b_re + a_im * b_im, a_im * b_re - a_re * b_im))
                energy.append(0.5 * (a_re * a_re + a_im * a_im + b_re * b_re + b_im * b_im))
            total = jnp.sum(energy[0] * power[0] + energy[1] * power[1])
            floor = 0.1 * (total / (side * side)) + 1e-05
            white = []
            for h in range(2):
                inverse = 1.0 / (energy[h] + floor)
                pair = [x * inverse for x in cross[h]]
                if h == 1:
                    pair = [jnp.where(edge, x, 0.0) for x in pair]
                white.append(pair)
            (p_re, p_im), (m_re, m_im) = white
            rhs = jnp.concatenate(
                [
                    jnp.concatenate([p_re + m_re, p_im + m_im], axis=1),
                    jnp.concatenate([m_im - p_im, p_re - m_re], axis=1),
                ],
                axis=0,
            ).astype(bf16)
            turned.append(mm(left_i[...], rhs))
        parts = front(i + 1)
        prior = None
        for r in range(group):
            lhs = jnp.concatenate([x[r * count : (r + 1) * count] for x in turned], axis=0).astype(bf16)
            got = mm(lhs, back_m[r])
            now = got[:, :LANES] if prior is None else prior + got[:, :LANES]
            for u, s in enumerate(ids):
                pix[pl.ds(s * chunks_all + r, count, stride=chunks), :] = now[u * count : (u + 1) * count]
            prior = got[:, LANES:]
        for u, s in enumerate(ids):
            pix[pl.ds(s * chunks_all + group, count, stride=chunks), :] = prior[u * count : (u + 1) * count]
        keep(parts)
        return carry

    for u in range(BATCH):
        fetch(0, u).start()
    keep(front(0))
    rounds = (used + BATCH - 1) // BATCH
    lax.fori_loop(0, rounds, batch, 0)
    for u in range(BATCH):
        fetch(rounds, u).wait()

    def put(g):
        mine = pl.ds(g * 16, 16)
        return pltpu.make_async_copy(flat.at[mine], out.at[mine], out_sem.at[g])

    for g in range(slots // 16):

        def gather(i, carry):
            for u in range(20):
                t = i * 20 + u
                at = pl.multiple_of(t * LANES, LANES)
                low = pix[pl.ds(g * 16 * chunks_all + t, 8, stride=chunks_all), :]
                high = pix[pl.ds((g * 16 + 8) * chunks_all + t, 8, stride=chunks_all), :]
                flat[g * 16 : g * 16 + 16, pl.ds(at, LANES)] = jnp.concatenate([low, high], axis=0).astype(bf16)
            return carry

        lax.fori_loop(0, chunks_all // 20, gather, 0)
        put(g).start()
    for g in range(slots // 16):
        put(g).wait()


def pack(cap, tall, owners, roots, offsets, cached, packed, ints, steps):
    held = owners.shape[1]
    i32 = jnp.int32
    peers = packed.shape[0]
    below = lax.broadcasted_iota(i32, (held, held), 0)
    across = lax.broadcasted_iota(i32, (held, held), 1)
    target = owners[...]
    column = jnp.sum(jnp.where(below == across, target, 0), axis=1, keepdims=True)
    rank = jnp.sum(((column == target) & (below < across)).astype(i32), axis=0, keepdims=True)

    def places(step):
        at = lax.broadcasted_iota(i32, (peers * step, held), 0)
        return at == target * step + rank

    tall_sel = places(tall)
    lane = lax.broadcasted_iota(i32, (peers * tall, LANES), 1)
    first, second = [
        jnp.sum(jnp.where(tall_sel, roots[a : a + 1, :], 0), axis=1, keepdims=True) for a in (0, 1)
    ]
    both = jnp.where(lane == 0, first, jnp.where(lane == 1, second, 0))
    ints[...] = both.reshape(ints.shape)
    lane = lax.broadcasted_iota(i32, steps.shape, 1)
    low = lax.broadcasted_iota(i32, steps.shape, 0)
    spread = jnp.where(lane == 0, offsets[:, :1], jnp.where(lane == 1, offsets[:, 1:2], 0))
    steps[...] = jnp.where(low == 0, spread, 0)
    selector = places(cap).astype(jnp.float32).astype(jnp.bfloat16)
    got = mm(selector, cached[...]).astype(packed.dtype)
    packed[...] = got.reshape(packed.shape)


def packed_all(owners, roots, offsets, cached, peers, cap, tall):
    held, area = cached.shape
    tile = 5 * 2 * LANES
    full = lambda *shape: pl.BlockSpec(shape, lambda i: (0,) * len(shape))
    return pl.pallas_call(
        functools.partial(pack, cap, tall),
        grid=(area // tile,),
        out_shape=[
            jax.ShapeDtypeStruct((peers, cap, area), cached.dtype),
            jax.ShapeDtypeStruct((peers, tall, LANES), jnp.int32),
            jax.ShapeDtypeStruct((8, LANES), jnp.int32),
        ],
        in_specs=[
            full(1, held), full(2, held), full(1, 2), pl.BlockSpec((held, tile), lambda i: (0, i)),
        ],
        out_specs=[
            pl.BlockSpec((peers, cap, tile), lambda i: (0, 0, i)), full(peers, tall, LANES), full(8, LANES),
        ],
        name="pack",
    )(owners, roots, offsets, cached)


def sharpened(packed, ints, steps, shard, layers):
    peers, cap, area = packed.shape
    slots = peers * cap
    side = math.isqrt(area)
    right, right_m, left_t, left_m, left_i, back_m, power = [jnp.asarray(x) for x in tables(side)]
    group, pad = right_m.shape[0], power.shape[1]
    count, chunks_all = side // group, area // LANES
    rows, width = shard.shape
    vmem = pl.BlockSpec(memory_space=pltpu.VMEM)
    smem = pl.BlockSpec(memory_space=pltpu.SMEM)
    hbm = pl.BlockSpec(memory_space=pl.ANY)
    dma = pltpu.SemaphoreType.DMA
    spec, anchor, ints_all, steps_all = pl.pallas_call(
        functools.partial(exchange, side, peers, layers, cap, chunks_all, group, count, pad),
        out_shape=[
            jax.ShapeDtypeStruct((slots, 4, pad, LANES), jnp.bfloat16),
            jax.ShapeDtypeStruct((layers, rows, width), shard.dtype),
            jax.ShapeDtypeStruct(ints.shape, ints.dtype),
            jax.ShapeDtypeStruct((layers,) + steps.shape, steps.dtype),
        ],
        in_specs=[vmem, hbm, hbm, hbm, vmem, vmem],
        out_specs=[hbm] * 4,
        scratch_shapes=[
            pltpu.VMEM(packed.shape, packed.dtype),
            pltpu.VMEM((cap * chunks_all, LANES), jnp.float32),
            pltpu.VMEM((slots, 4, pad, LANES), jnp.bfloat16),
            dma((peers,)),
            dma((peers - 1,)), dma((peers - 1,)), dma((peers - 1,)), dma((peers - 1,)),
            dma((layers - 1,)), dma((layers - 1,)), dma((layers - 1,)), dma((layers - 1,)),
            dma((layers - 1,)), dma((layers - 1,)), dma((4,)),
        ],
        compiler_params=pltpu.CompilerParams(vmem_limit_bytes=48 << 20, collective_id=0, has_side_effects=True),
        name="exchange",
    )(packed, ints, steps, shard, right_m, left_m)
    return pl.pallas_call(
        functools.partial(correlate, side, slots, cap, layers, chunks_all, group, count, pad),
        out_shape=jax.ShapeDtypeStruct((slots, area), jnp.bfloat16),
        in_specs=[smem, smem, hbm] + [vmem] * 6,
        out_specs=hbm,
        scratch_shapes=[
            pltpu.VMEM(((slots + 1) * chunks_all, LANES), jnp.float32),
            pltpu.VMEM((layers * rows * width // LANES, LANES), jnp.float32),
            pltpu.VMEM((BATCH, 4, pad, LANES), jnp.float32),
            pltpu.VMEM((2, BATCH, 4, pad, LANES), jnp.bfloat16),
            pltpu.VMEM((slots, area), jnp.bfloat16),
            pltpu.SMEM((slots + 2 * BATCH + 1,), jnp.int32),
            pltpu.SMEM((slots + 1,), jnp.int32),
            dma((2, BATCH)),
            dma((slots // 16,)),
        ],
        compiler_params=pltpu.CompilerParams(vmem_limit_bytes=48 << 20),
        name="correlate",
    )(
        ints_all.reshape(-1, LANES), steps_all.reshape(-1, LANES), spec,
        anchor.reshape(layers * rows, width), right, left_t, left_i, back_m, power,
    )


def body(rendered, cached, owners, roots, offsets):
    area = cached.shape[2]
    held = cached.shape[1]
    owner_count = lax.axis_size("tile")
    capacity = max(2, 2 * held // owner_count)
    tall = -(-capacity // 8) * 8
    packed, ints, steps = packed_all(
        owners[:, :, 0], roots[0].T, offsets, cached[0], owner_count, capacity, tall
    )
    result = sharpened(packed, ints, steps, rendered[0], lax.axis_size("sec"))
    return result.reshape(1, 1, owner_count, capacity, area)


def solution(mesh):
    placed = (
        P("tile", "sec", None),
        P("sec", "tile", None),
        P("sec", "tile", None),
        P("sec", "tile", None),
        P("sec", None),
    )
    return jax.shard_map(
        body,
        mesh=mesh,
        in_specs=placed,
        out_specs=P("sec", "tile", None, None, None),
        check_vma=False,
    )
```

```python
import functools
import math

import jax
import jax.numpy as jnp
import ml_dtypes
import numpy as np
from jax import lax
from jax.experimental import pallas as pl
from jax.experimental.pallas import tpu as pltpu
from jax.sharding import PartitionSpec as P

LANES = 128
BATCH = 8
MESH = pl.DeviceIdType.MESH


def tables(side):
    half = side // 2 + 1
    pad = -(-half // 8) * 8
    group = side // 32 - 1
    count = side // group
    full = np.arange(side)
    low = np.arange(half)
    phase = (full[:, None] * low[None, :] % side).astype(np.float32) * np.float32(2.0 * math.pi / side)
    cos = np.cos(phase).astype(ml_dtypes.bfloat16)
    sin = np.sin(phase).astype(ml_dtypes.bfloat16)
    counts = np.where((low == 0) | (low == side // 2), 1.0, 2.0).astype(np.float32)
    right = np.zeros((side, 2 * LANES), ml_dtypes.bfloat16)
    right[:, :half] = cos
    right[:, LANES : LANES + half] = -sin
    back = np.zeros((2 * LANES, side), ml_dtypes.bfloat16)
    scaled = counts[:, None] / np.float32(side)
    back[:half] = (scaled * np.cos(phase).T).astype(ml_dtypes.bfloat16)
    back[LANES : LANES + half] = (-scaled * np.sin(phase).T).astype(ml_dtypes.bfloat16)
    order = (np.arange(count)[None, :] * group + np.arange(group)[:, None]).reshape(-1)
    left_t = np.zeros((2 * pad, side), ml_dtypes.bfloat16)
    left_t[:half] = cos.T
    left_t[pad : pad + half] = sin.T
    left_m = left_t[:, order]
    left_i = left_m.T.copy()
    right_m = np.zeros((group, 2 * LANES, 2 * LANES), ml_dtypes.bfloat16)
    back_m = np.zeros((group, 2 * LANES, 2 * LANES), ml_dtypes.bfloat16)
    for r in range(group):
        at = side * r - LANES * r
        right_m[r, at : at + side] = right
        back_m[r, :, at : at + side] = back
    power = np.zeros((2, pad, LANES), np.float32)
    power[:, :half, :half] = counts[None, None, :]
    power[1, 0] = 0.0
    power[1, side // 2] = 0.0
    return right, right_m, left_t, left_m, left_i, back_m, power


def mm(a, b):
    return jnp.dot(a, b, preferred_element_type=jnp.float32)


def halves(left, segment, pad, kind=jnp.bfloat16):
    both = mm(left, segment)
    p_re, p_im = both[:pad, :LANES], both[:pad, LANES:]
    q_re, q_im = both[pad:, :LANES], both[pad:, LANES:]
    return [x.astype(kind) for x in (p_re + q_im, p_im - q_re, p_re - q_im, p_im + q_re)]


def flipped(place, step, bits):
    total = 0
    for b in range(bits):
        total = total + (place // (1 << b) + step // (1 << b)) % 2 * (1 << b)
    return total


def exchange(side, peers, layers, cap, chunks_all, group, count, pad,
             packed, ints, steps, shard, right_m, left_m,
             spec, anchor, ints_out, steps_out,
             landed, pix, made, made_sem, blk_send, blk_recv, int_send, int_recv,
             up_send, up_recv, down_send, down_recv, off_send, off_recv, own_sem):
    bf16 = jnp.bfloat16
    layer, me = lax.axis_index("sec"), lax.axis_index("tile")
    bits = peers.bit_length() - 1
    chunks = group + 1
    barrier = pltpu.get_barrier_semaphore()
    for d in range(1, peers):
        pl.semaphore_signal(barrier, inc=1, device_id=(layer, flipped(me, d, bits)), device_id_type=MESH)
    for d in range(1, layers):
        pl.semaphore_signal(barrier, inc=1, device_id=((layer + d) % layers, me), device_id_type=MESH)
    pl.semaphore_wait(barrier, peers + layers - 2)

    def relay(up, k):
        which = layer - k if up else layer + k
        which = jnp.clip(which, 0, layers - 1)
        return pltpu.make_async_remote_copy(
            src_ref=shard if k == 0 else anchor.at[which],
            dst_ref=anchor.at[which],
            send_sem=(up_send if up else down_send).at[k],
            recv_sem=(up_recv if up else down_recv).at[k],
            device_id=((layer + 1) % layers if up else (layer + layers - 1) % layers, me),
            device_id_type=MESH,
        )

    def sends(up, k):
        return (layer < layers - 1) & (layer >= k) if up else (layer > 0) & (layer + k <= layers - 1)

    def gets(up, k):
        return (layer - 1 >= k) if up else (layer + 1 + k <= layers - 1)

    def start_relay(k):
        for up in (True, False):
            @pl.when(sends(up, k))
            def _():
                relay(up, k).start()

    def block(d):
        other = flipped(me, d, bits)
        return pltpu.make_async_remote_copy(
            src_ref=packed.at[other], dst_ref=landed.at[me],
            send_sem=blk_send.at[d - 1], recv_sem=blk_recv.at[d - 1],
            device_id=(layer, other), device_id_type=MESH,
        )

    def small(d):
        other = flipped(me, d, bits)
        return pltpu.make_async_remote_copy(
            src_ref=ints.at[other], dst_ref=ints_out.at[me],
            send_sem=int_send.at[d - 1], recv_sem=int_recv.at[d - 1],
            device_id=(layer, other), device_id_type=MESH,
        )

    def offset(d):
        return pltpu.make_async_remote_copy(
            src_ref=steps, dst_ref=steps_out.at[layer],
            send_sem=off_send.at[d - 1], recv_sem=off_recv.at[d - 1],
            device_id=((layer + d) % layers, me), device_id_type=MESH,
        )

    start_relay(0)
    for d in range(1, peers):
        block(d).start()
    for d in range(1, peers):
        small(d).start()
    for d in range(1, layers):
        offset(d).start()
    own = [
        pltpu.make_async_copy(packed.at[me], landed.at[me], own_sem.at[0]),
        pltpu.make_async_copy(ints.at[me], ints_out.at[me], own_sem.at[1]),
        pltpu.make_async_copy(steps, steps_out.at[layer], own_sem.at[2]),
        pltpu.make_async_copy(shard, anchor.at[layer], own_sem.at[3]),
    ]
    for x in own:
        x.start()
    own[0].wait()

    some = min(BATCH, cap)

    def put(d):
        mine = pl.ds(flipped(me, d, bits) * cap, cap)
        return pltpu.make_async_copy(made.at[mine], spec.at[mine], made_sem.at[d])

    def process(d, carry):
        source = flipped(me, d, bits)

        def spread(i, inner):
            for u in range(8):
                t = i * 8 + u
                at = pl.multiple_of(t * LANES, LANES)
                pix[pl.ds(t, cap, stride=chunks_all), :] = landed[source, :, pl.ds(at, LANES)].astype(jnp.float32)
            return inner

        lax.fori_loop(0, chunks_all // 8, spread, 0)
        for first in range(0, cap, some):
            pieces = [
                [pix[pl.ds((first + u) * chunks_all + q, count, stride=chunks), :] for q in range(chunks)]
                for u in range(some)
            ]
            seg = []
            for r in range(group):
                lhs = jnp.concatenate(
                    [jnp.concatenate([x[r], x[r + 1]], axis=1) for x in pieces], axis=0
                ).astype(bf16)
                seg.append(mm(lhs, right_m[r]))
            for u in range(some):
                one = jnp.concatenate([x[u * count : (u + 1) * count] for x in seg], axis=0).astype(bf16)
                for h, part in enumerate(halves(left_m[...], one, pad)):
                    made[source * cap + first + u, h] = part
        put(d).start()
        return carry

    def step(d, carry):
        block(d).wait_recv()
        return process(d, carry)

    process(0, 0)
    cuts = [1 + (peers - 1) * i // (layers - 1) for i in range(layers)]
    for k in range(layers - 1):
        lax.fori_loop(cuts[k], cuts[k + 1], step, 0)
        for up in (True, False):
            @pl.when(gets(up, k))
            def _():
                relay(up, k).wait_recv()
        if k < layers - 2:
            start_relay(k + 1)
    for k in range(layers - 1):
        for up in (True, False):
            @pl.when(sends(up, k))
            def _():
                relay(up, k).wait_send()
    for d in range(1, peers):
        block(d).wait_send()
        small(d).wait()
    for d in range(1, layers):
        offset(d).wait()
    for x in own[1:]:
        x.wait()
    for d in range(peers):
        put(d).wait()


def correlate(side, slots, cap, layers, chunks_all, group, count, pad, ints, steps, spec_in, anchor_in, right,
              left_t, left_i, back_m, power, out, pix, anchor, ahead, spec, flat, todo, rest, in_sem, out_sem):
    chunks = group + 1
    f32, bf16 = jnp.float32, jnp.bfloat16
    rows_in, width = anchor_in.shape
    layer = lax.axis_index("sec")
    tall = ints.shape[0] * cap // slots
    drift = [sum(jnp.where(z <= layer, steps[z * steps.shape[0] // layers, a], 0) for z in range(layers)) for a in (0, 1)]

    def widen(i, carry):
        at = pl.multiple_of(i * 32, 32)
        for c in range(width // LANES):
            wide = anchor_in[pl.ds(at, 32), c * LANES : (c + 1) * LANES].astype(f32)
            anchor[pl.ds(at + c * rows_in, 32), :] = wide
        return carry

    lax.fori_loop(0, rows_in // 32, widen, 0)

    def root(i, a):
        return ints[i // cap * tall + lax.rem(i, cap), a]

    def listed(i, used):
        for u in range(8):
            here = i * 8 + u
            todo[used] = here
            rest[here - used] = here
            used = used + (root(here, 0) > 0).astype(jnp.int32)
        return used

    used = lax.fori_loop(0, slots // 8, listed, jnp.int32(0))

    def clear(i, carry):
        pix[pl.ds(rest[i] * chunks_all, chunks_all), :] = jnp.zeros((chunks_all, LANES), f32)
        return carry

    lax.fori_loop(0, slots - used, clear, 0)
    for u in range(2 * BATCH):
        todo[used + u] = slots

    lane = lax.broadcasted_iota(jnp.int32, (side, LANES), 1)
    at_row = lax.broadcasted_iota(jnp.int32, (pad, LANES), 0)
    edge = (at_row != 0) & (at_row != side // 2)

    def window(here):
        row = jnp.clip(root(here, 0) + drift[0], 0, rows_in - side)
        col = jnp.clip(root(here, 1) + drift[1], 0, width - side)
        chunk = col // LANES
        off = col - chunk * LANES
        turn = lax.rem(LANES - off, LANES)
        pieces = []
        for u in range(3):
            at = jnp.minimum(chunk + u, width // LANES - 1) * rows_in + row
            pieces.append(pltpu.roll(anchor[pl.ds(at, side), :], turn, 1))
        keep = lane < LANES - off
        first = jnp.where(keep, pieces[0], pieces[1])
        second = jnp.where(keep, pieces[1], pieces[2])
        return jnp.concatenate([first, second], axis=1)[:, :side].astype(bf16)

    def fetch(i, u):
        place = lax.rem(i, 2)
        slot = jnp.minimum(todo[i * BATCH + u], slots - 1)
        return pltpu.make_async_copy(spec_in.at[slot], spec.at[place, u], in_sem.at[place, u])

    def front(i):
        safe = [jnp.minimum(todo[i * BATCH + u], slots - 1) for u in range(BATCH)]
        wins = jnp.concatenate([window(s) for s in safe], axis=0)
        seg_t = mm(wins, right[...]).astype(bf16)
        return [halves(left_t[...], seg_t[u * side : (u + 1) * side], pad, f32) for u in range(BATCH)]

    def keep(parts):
        for u in range(BATCH):
            for h in range(4):
                ahead[u, h] = parts[u][h]

    def batch(i, carry):
        ids = [todo[i * BATCH + u] for u in range(BATCH)]
        for u in range(BATCH):
            fetch(i + 1, u).start()
        for u in range(BATCH):
            fetch(i, u).wait()
        place = lax.rem(i, 2)
        turned = []
        for u in range(BATCH):
            move = [spec[place, u, h].astype(f32) for h in range(4)]
            tmpl = [ahead[u, h] for h in range(4)]
            energy, cross = [], []
            for h in range(2):
                a_re, a_im = move[2 * h], move[2 * h + 1]
                b_re, b_im = tmpl[2 * h], tmpl[2 * h + 1]
                cross.append((a_re * b_re + a_im * b_im, a_im * b_re - a_re * b_im))
                energy.append(0.5 * (a_re * a_re + a_im * a_im + b_re * b_re + b_im * b_im))
            total = jnp.sum(energy[0] * power[0] + energy[1] * power[1])
            floor = 0.1 * (total / (side * side)) + 1e-05
            white = []
            for h in range(2):
                inverse = 1.0 / (energy[h] + floor)
                pair = [x * inverse for x in cross[h]]
                if h == 1:
                    pair = [jnp.where(edge, x, 0.0) for x in pair]
                white.append(pair)
            (p_re, p_im), (m_re, m_im) = white
            rhs = jnp.concatenate(
                [
                    jnp.concatenate([p_re + m_re, p_im + m_im], axis=1),
                    jnp.concatenate([m_im - p_im, p_re - m_re], axis=1),
                ],
                axis=0,
            ).astype(bf16)
            turned.append(mm(left_i[...], rhs))
        parts = front(i + 1)
        prior = None
        for r in range(group):
            lhs = jnp.concatenate([x[r * count : (r + 1) * count] for x in turned], axis=0).astype(bf16)
            got = mm(lhs, back_m[r])
            now = got[:, :LANES] if prior is None else prior + got[:, :LANES]
            for u, s in enumerate(ids):
                pix[pl.ds(s * chunks_all + r, count, stride=chunks), :] = now[u * count : (u + 1) * count]
            prior = got[:, LANES:]
        for u, s in enumerate(ids):
            pix[pl.ds(s * chunks_all + group, count, stride=chunks), :] = prior[u * count : (u + 1) * count]
        keep(parts)
        return carry

    for u in range(BATCH):
        fetch(0, u).start()
    keep(front(0))
    rounds = (used + BATCH - 1) // BATCH
    lax.fori_loop(0, rounds, batch, 0)
    for u in range(BATCH):
        fetch(rounds, u).wait()

    def put(g):
        mine = pl.ds(g * 16, 16)
        return pltpu.make_async_copy(flat.at[mine], out.at[mine], out_sem.at[g])

    for g in range(slots // 16):

        def gather(i, carry):
            for u in range(20):
                t = i * 20 + u
                at = pl.multiple_of(t * LANES, LANES)
                low = pix[pl.ds(g * 16 * chunks_all + t, 8, stride=chunks_all), :]
                high = pix[pl.ds((g * 16 + 8) * chunks_all + t, 8, stride=chunks_all), :]
                flat[g * 16 : g * 16 + 16, pl.ds(at, LANES)] = jnp.concatenate([low, high], axis=0).astype(bf16)
            return carry

        lax.fori_loop(0, chunks_all // 20, gather, 0)
        put(g).start()
    for g in range(slots // 16):
        put(g).wait()


def pack(cap, tall, owners, roots, offsets, cached, packed, ints, steps, selector):
    @pl.when(pl.program_id(0) == 0)
    def _():
        held = owners.shape[1]
        i32 = jnp.int32
        peers = packed.shape[0]
        below = lax.broadcasted_iota(i32, (held, held), 0)
        across = lax.broadcasted_iota(i32, (held, held), 1)
        target = owners[...]
        column = jnp.sum(jnp.where(below == across, target, 0), axis=1, keepdims=True)
        rank = jnp.sum(((column == target) & (below < across)).astype(i32), axis=0, keepdims=True)

        def places(step):
            at = lax.broadcasted_iota(i32, (peers * step, held), 0)
            return at == target * step + rank

        tall_sel = places(tall)
        lane = lax.broadcasted_iota(i32, (peers * tall, LANES), 1)
        first, second = [
            jnp.sum(jnp.where(tall_sel, roots[a : a + 1, :], 0), axis=1, keepdims=True) for a in (0, 1)
        ]
        both = jnp.where(lane == 0, first, jnp.where(lane == 1, second, 0))
        ints[...] = both.reshape(ints.shape)
        lane = lax.broadcasted_iota(i32, steps.shape, 1)
        low = lax.broadcasted_iota(i32, steps.shape, 0)
        spread = jnp.where(lane == 0, offsets[:, :1], jnp.where(lane == 1, offsets[:, 1:2], 0))
        steps[...] = jnp.where(low == 0, spread, 0)
        selector[...] = places(cap).astype(jnp.float32).astype(jnp.bfloat16)

    got = mm(selector[...], cached[...]).astype(packed.dtype)
    packed[...] = got.reshape(packed.shape)


def packed_all(owners, roots, offsets, cached, peers, cap, tall):
    held, area = cached.shape
    tile = 20 * 2 * LANES
    full = lambda *shape: pl.BlockSpec(shape, lambda i: (0,) * len(shape))
    return pl.pallas_call(
        functools.partial(pack, cap, tall),
        grid=(area // tile,),
        out_shape=[
            jax.ShapeDtypeStruct((peers, cap, area), cached.dtype),
            jax.ShapeDtypeStruct((peers, tall, LANES), jnp.int32),
            jax.ShapeDtypeStruct((8, LANES), jnp.int32),
        ],
        in_specs=[
            full(1, held), full(2, held), full(1, 2), pl.BlockSpec((held, tile), lambda i: (0, i)),
        ],
        out_specs=[
            pl.BlockSpec((peers, cap, tile), lambda i: (0, 0, i)), full(peers, tall, LANES), full(8, LANES),
        ],
        scratch_shapes=[pltpu.VMEM((peers * cap, held), jnp.bfloat16)],
        name="pack",
    )(owners, roots, offsets, cached)


def sharpened(packed, ints, steps, shard, layers):
    peers, cap, area = packed.shape
    slots = peers * cap
    side = math.isqrt(area)
    right, right_m, left_t, left_m, left_i, back_m, power = [jnp.asarray(x) for x in tables(side)]
    group, pad = right_m.shape[0], power.shape[1]
    count, chunks_all = side // group, area // LANES
    rows, width = shard.shape
    vmem = pl.BlockSpec(memory_space=pltpu.VMEM)
    smem = pl.BlockSpec(memory_space=pltpu.SMEM)
    hbm = pl.BlockSpec(memory_space=pl.ANY)
    dma = pltpu.SemaphoreType.DMA
    spec, anchor, ints_all, steps_all = pl.pallas_call(
        functools.partial(exchange, side, peers, layers, cap, chunks_all, group, count, pad),
        out_shape=[
            jax.ShapeDtypeStruct((slots, 4, pad, LANES), jnp.bfloat16),
            jax.ShapeDtypeStruct((layers, rows, width), shard.dtype),
            jax.ShapeDtypeStruct(ints.shape, ints.dtype),
            jax.ShapeDtypeStruct((layers,) + steps.shape, steps.dtype),
        ],
        in_specs=[vmem, hbm, hbm, hbm, vmem, vmem],
        out_specs=[hbm] * 4,
        scratch_shapes=[
            pltpu.VMEM(packed.shape, packed.dtype),
            pltpu.VMEM((cap * chunks_all, LANES), jnp.float32),
            pltpu.VMEM((slots, 4, pad, LANES), jnp.bfloat16),
            dma((peers,)),
            dma((peers - 1,)), dma((peers - 1,)), dma((peers - 1,)), dma((peers - 1,)),
            dma((layers - 1,)), dma((layers - 1,)), dma((layers - 1,)), dma((layers - 1,)),
            dma((layers - 1,)), dma((layers - 1,)), dma((4,)),
        ],
        compiler_params=pltpu.CompilerParams(vmem_limit_bytes=48 << 20, collective_id=0, has_side_effects=True),
        name="exchange",
    )(packed, ints, steps, shard, right_m, left_m)
    return pl.pallas_call(
        functools.partial(correlate, side, slots, cap, layers, chunks_all, group, count, pad),
        out_shape=jax.ShapeDtypeStruct((slots, area), jnp.bfloat16),
        in_specs=[smem, smem, hbm] + [vmem] * 6,
        out_specs=hbm,
        scratch_shapes=[
            pltpu.VMEM(((slots + 1) * chunks_all, LANES), jnp.float32),
            pltpu.VMEM((layers * rows * width // LANES, LANES), jnp.float32),
            pltpu.VMEM((BATCH, 4, pad, LANES), jnp.float32),
            pltpu.VMEM((2, BATCH, 4, pad, LANES), jnp.bfloat16),
            pltpu.VMEM((slots, area), jnp.bfloat16),
            pltpu.SMEM((slots + 2 * BATCH + 1,), jnp.int32),
            pltpu.SMEM((slots + 1,), jnp.int32),
            dma((2, BATCH)),
            dma((slots // 16,)),
        ],
        compiler_params=pltpu.CompilerParams(vmem_limit_bytes=48 << 20),
        name="correlate",
    )(
        ints_all.reshape(-1, LANES), steps_all.reshape(-1, LANES), spec,
        anchor.reshape(layers * rows, width), right, left_t, left_i, back_m, power,
    )


def body(rendered, cached, owners, roots, offsets):
    area = cached.shape[2]
    held = cached.shape[1]
    owner_count = lax.axis_size("tile")
    capacity = max(2, 2 * held // owner_count)
    tall = -(-capacity // 8) * 8
    packed, ints, steps = packed_all(
        owners[:, :, 0], roots[0].T, offsets, cached[0], owner_count, capacity, tall
    )
    result = sharpened(packed, ints, steps, rendered[0], lax.axis_size("sec"))
    return result.reshape(1, 1, owner_count, capacity, area)


def solution(mesh):
    placed = (
        P("tile", "sec", None),
        P("sec", "tile", None),
        P("sec", "tile", None),
        P("sec", "tile", None),
        P("sec", None),
    )
    return jax.shard_map(
        body,
        mesh=mesh,
        in_specs=placed,
        out_specs=P("sec", "tile", None, None, None),
        check_vma=False,
    )
```
